32 devices in a mesh: ctx: 8 (over z, x), head: 4 (over y, core).
Axes of the slice: x: 2, y: 2, z: 4, core: 2. Of those that a mesh axis runs over, the one named last changes fastest.
Arguments:
- query: bfloat16 [16384, 8192], P(('ctx', 'head')), as said below
- key: bfloat16 [16384, 1024], P(('ctx', 'head')), as said below
- value: bfloat16 [16384, 1024], P(('ctx', 'head')), may hold values from -6 to 6
- doc_ids: int32 [128], replicated, may hold values from 0 to 20, never falling along the last dimension, each value on 1 to 8 neighbouring positions
- plan: int32 [128], replicated, may hold values from 0 to 127, as said below
Outputs:
- attended: bfloat16 [16384, 8192], P('ctx', 'head')
The draws below stay inside these ranges and needn't reach their ends.
Inputs may be any that keep to these rules, and one draw needn't show every extreme that they name: `doc_ids`: block ids never fall; each document holds 1 to 8 blocks, one exactly 8. `plan`: A permutation of the 128 blocks. Output positions k * 16 to (k + 1) * 16 - 1 belong to context shard k. Every shard receives 16 blocks; of the blocks j * 16 to (j + 1) * 16 - 1 at most 2 go to one shard, and exactly 2 to some shard. `query`: real values; no structure promised. `key`: real values; no structure promised.
All inputs are finite; a program needn't handle non-finite values.
Results may differ from the reference program's by a relative error of at most 0.0038.
Values may be sent and summed in bfloat16 or wider, within the bound.
A program may use at most 128 MiB of HBM per device.

```python
import math
import jax
import jax.numpy as jnp
import numpy as np
from jax import lax

HQ = 64
HK = 8
HD = 128
BLK = 128
BLK_DEV = 16
MAXDOC = 8
NBLK = 128
TOKENS = 16384
NDOC = 21


def key_field(key):
    base = jax.random.fold_in(key, 11)
    first = jax.random.fold_in(base, 0)
    field = jax.random.normal(first, (TOKENS, HK * HD), jnp.float32)
    marks = jnp.zeros((TOKENS,), bool)
    return (field, marks)


def draw_key(key, part):
    field, marks = key_field(key)
    return field.astype(jnp.bfloat16)


def draw_query(key, part):
    field, marks = key_field(key)
    noise_key = jax.random.fold_in(key, 12)
    noise = jax.random.normal(noise_key, (TOKENS, HQ * HD), jnp.float32)
    return jnp.where(marks[:, None], noise, noise).astype(jnp.bfloat16)


def draw_plan(key, part):
    base = jax.random.fold_in(key, 21)
    first, second, third, fourth = jax.random.split(base, 4)
    shards = NBLK // BLK_DEV
    ranks = jax.random.permutation(first, shards)
    offsets = ranks[jnp.arange(BLK_DEV) % shards]
    sigma = jax.random.permutation(second, shards)
    raw = jax.random.randint(third, (shards, BLK_DEV), 0, 1048576) * BLK_DEV + jnp.arange(BLK_DEV)[None, :]
    local_order = jnp.argsort(raw, axis=1, stable=True)
    sources = jnp.arange(shards)[:, None]
    target = sigma[(sources + offsets[local_order]) % shards]
    mixing = jax.random.permutation(fourth, NBLK)
    sort_key = target.reshape(NBLK) * NBLK + mixing
    return jnp.argsort(sort_key, stable=True).astype(jnp.int32)


def steps_of(stream_key, dims, cuts, low, high):
    def one(axis_at, blocks):
        draws = jax.random.uniform(jax.random.fold_in(jax.random.fold_in(stream_key, 6), axis_at), (blocks,), jnp.float32, low / len(cuts), high / len(cuts))
        return jnp.repeat(jnp.exp(draws), dims[axis_at] // blocks).reshape((-1,) + (1,) * (len(dims) - axis_at - 1))

    factor_of = one(*cuts[0])
    for cut in cuts[1:]:
        factor_of = factor_of * one(*cut)
    return factor_of


def length_profile(number_of, total, reach, lean):
    weights = [(1 << 20) // math.isqrt(rank ** lean) + 1 for rank in range(2, number_of + 1)]
    surplus, counts = total - reach - (number_of - 1), [1] * (number_of - 1)
    while surplus > 0:
        free = [i for i in range(number_of - 1) if counts[i] < reach]
        whole, budget = sum([weights[i] for i in free]), surplus
        for i in free:
            extra = min(reach - counts[i], max(1, budget * weights[i] // whole), surplus)
            counts[i] = counts[i] + extra
            surplus = surplus - extra
    return np.array([reach] + counts)


def uneven(rng, number_of, total, bound, lean):
    if number_of == 2:
        one = jax.random.randint(rng, (), max(1, total - bound), min(bound, total - 1) + 1)
        return jnp.stack([one, total - one])
    tallies = jnp.asarray(length_profile(number_of, total, bound, lean), jnp.int32)
    pairs = (number_of - 1) // 2
    giver, receiver = tallies[1:1 + 2 * pairs:2], tallies[2:2 + 2 * pairs:2]
    slack = jnp.minimum(giver - 1, bound - receiver)
    moved = jax.random.randint(jax.random.fold_in(rng, 1), (pairs,), 0, 1 << 20) % (slack + 1)
    tallies = tallies.at[1:1 + 2 * pairs:2].set(giver - moved).at[2:2 + 2 * pairs:2].set(receiver + moved)
    return tallies[jax.random.permutation(jax.random.fold_in(rng, 2), number_of)]


def bell_draw(key, extent, scale, most, cuts=(), held_as=jnp.bfloat16):
    drawn = jax.random.normal(key, extent, jnp.float32) * scale
    if len(cuts) > 0:
        drawn = steps_of(key, extent, cuts, -0.22, 0.18) * drawn
    return jnp.clip(drawn, min=-most, max=most).astype(held_as)


def setup_inputs(seed: int = 0) -> dict:
    streams_of = jax.random.split(jax.random.key(seed), 6)
    return {
        "query": draw_query(jax.random.fold_in(streams_of[5], 71), 0),
        "key": draw_key(jax.random.fold_in(streams_of[5], 71), 0),
        "value": bell_draw(streams_of[2], (TOKENS, HK * HD), 1.0, 6.0, ((0, 32),)),
        "doc_ids": jnp.searchsorted(jnp.cumsum(uneven(streams_of[3], NDOC, NBLK, MAXDOC, 2)), jnp.arange(NBLK), side="right").astype(jnp.int32),
        "plan": draw_plan(jax.random.fold_in(streams_of[5], 71), 0),
    }


def reference(query, key, value, doc_ids, plan):
    width = HQ * HD
    group = HQ // HK
    window = MAXDOC * BLK
    pad = (MAXDOC - 1) * BLK
    scale = 1.0 / math.sqrt(HD)
    key_pad = jnp.concatenate([jnp.zeros((pad, HK * HD), key.dtype), key], 0)
    value_pad = jnp.concatenate([jnp.zeros((pad, HK * HD), value.dtype), value], 0)
    row_docs = jnp.repeat(doc_ids, BLK)
    doc_pad = jnp.concatenate([jnp.full((pad,), -1, jnp.int32), row_docs.astype(jnp.int32)], 0)

    def one_block(block):
        start = (block * BLK).astype(jnp.int32)
        queries = lax.dynamic_slice_in_dim(query, start, BLK, 0).astype(jnp.float32).reshape(BLK, HK, group, HD)
        keys = lax.dynamic_slice_in_dim(key_pad, start, window, 0).astype(jnp.float32).reshape(window, HK, HD)
        values = lax.dynamic_slice_in_dim(value_pad, start, window, 0).astype(jnp.float32).reshape(window, HK, HD)
        docs = lax.dynamic_slice_in_dim(doc_pad, start, window, 0)
        scores = jnp.einsum('qkgd,skd->kgqs', queries, keys) * scale
        query_pos = start + jnp.arange(BLK, dtype=jnp.int32)
        key_pos = start - pad + jnp.arange(window, dtype=jnp.int32)
        allowed = (docs[None, :] == doc_ids[block]) & (key_pos[None, :] <= query_pos[:, None])
        scores = jnp.where(allowed, scores, -jnp.inf)
        top = lax.optimization_barrier(jnp.max(scores, axis=3, keepdims=True))
        expo = jnp.exp(scores - top)
        total = lax.optimization_barrier(jnp.sum(expo, axis=3))
        weights = lax.optimization_barrier(expo.astype(jnp.bfloat16)).astype(jnp.float32)
        summed = jnp.einsum('kgqs,skd->kgqd', weights, values)
        mixed = summed / total[..., None]
        return mixed.transpose(2, 0, 1, 3).reshape(BLK, width).astype(jnp.bfloat16)
    heads_out = lax.map(one_block, jnp.arange(NBLK, dtype=jnp.int32))
    return heads_out[plan].reshape(TOKENS, width)
```

```python
import functools
import math

import jax
import jax.numpy as jnp
from jax import lax
from jax.experimental import pallas as pl
from jax.experimental.pallas import tpu as pltpu
from jax.sharding import PartitionSpec as P

HD = 128
BLK = 128
MAXDOC = 8
HALO = (MAXDOC - 1) * BLK
MESH = pl.DeviceIdType.MESH


def aligned(x):
    return pl.multiple_of(x, BLK)


def fused_kernel(
    kv_heads, cap, slot_block, slot_count, q_ref, k_ref, v_ref, got_ref, *rest
):
    keys_in = rest[:kv_heads]
    values_in = rest[kv_heads : 2 * kv_heads]
    q_in, q_work, turned, v_work, out = rest[2 * kv_heads : 2 * kv_heads + 5]
    sems = rest[2 * kv_heads + 5 :]
    q_sent, q_got, kv_sent, kv_got, halo_sent, halo_got, out_sent, out_got, own_done = sems
    c, h = lax.axis_index("ctx"), lax.axis_index("head")
    nc, nh = lax.axis_size("ctx"), lax.axis_size("head")
    part = q_ref.shape[0]
    rows = nh * part
    blocks = rows // BLK
    heads = q_in.shape[0]
    group = heads // kv_heads
    factor = math.log2(math.e) / math.sqrt(HD)

    barrier = pltpu.get_barrier_semaphore()
    for d in range(1, nh):
        pl.semaphore_signal(
            barrier, inc=1, device_id=(c, lax.rem(h + d, nh)), device_id_type=MESH
        )
    for d in range(1, nc):
        pl.semaphore_signal(
            barrier, inc=1, device_id=(lax.rem(c + d, nc), h), device_id_type=MESH
        )
    pl.semaphore_wait(barrier, nh + nc - 2)

    my_rows = pl.ds(aligned(h * part), part)
    my_kv_rows = pl.ds(aligned(HALO + h * part), part)

    def send_kv(g):
        for at, (src, dst) in enumerate(((k_ref, keys_in[g]), (v_ref, values_in[g]))):
            for d in range(1, nh):
                t = lax.rem(h + d, nh)
                pltpu.make_async_remote_copy(
                    src_ref=src.at[:, pl.ds(aligned((t * kv_heads + g) * HD), HD)],
                    dst_ref=dst.at[my_kv_rows],
                    send_sem=kv_sent.at[g, at, d],
                    recv_sem=kv_got.at[g, at, h],
                    device_id=(c, t),
                    device_id_type=MESH,
                ).start()
            pltpu.make_async_copy(
                src.at[:, pl.ds(aligned((h * kv_heads + g) * HD), HD)],
                dst.at[my_kv_rows],
                kv_got.at[g, at, h],
            ).start()

    def send_q(k):
        for d in range(1, nh):
            t = lax.rem(h + d, nh)
            pltpu.make_async_remote_copy(
                src_ref=q_ref.at[:, pl.ds(aligned((t * heads + k) * HD), HD)],
                dst_ref=q_in.at[k, my_rows],
                send_sem=q_sent.at[k, d],
                recv_sem=q_got.at[k, h],
                device_id=(c, t),
                device_id_type=MESH,
            ).start()
        pltpu.make_async_copy(
            q_ref.at[:, pl.ds(aligned((h * heads + k) * HD), HD)],
            q_in.at[k, my_rows],
            q_got.at[k, h],
        ).start()

    def wait_on(ref, sem):
        pltpu.make_async_copy(ref, ref, sem).wait()

    def send_q_loop(k, carry):
        send_q(k)
        return carry

    send_kv(0)
    send_q(0)
    for g in range(1, kv_heads):
        send_kv(g)
    lax.fori_loop(1, heads, send_q_loop, 0)

    pieces = []
    for j in range(nh - 1, -1, -1):
        low, high = max(rows - HALO, j * part), (j + 1) * part
        if low < high:
            pieces.append((j, low, high - low))

    def halo_copy(g, at, p):
        ref = (keys_in[g], values_in[g])[at]
        _, low, size = pieces[p]
        return pltpu.make_async_remote_copy(
            src_ref=ref.at[pl.ds(HALO + low, size)],
            dst_ref=ref.at[pl.ds(HALO + low - rows, size)],
            send_sem=halo_sent.at[g, at, p],
            recv_sem=halo_got.at[g, at, p],
            device_id=(jnp.minimum(c + 1, nc - 1), h),
            device_id_type=MESH,
        )

    def gather_kv(g):
        waited = set()

        def wait_part(at, j):
            if (at, j) not in waited:
                waited.add((at, j))
                ref = (keys_in[g], values_in[g])[at]
                wait_on(ref.at[pl.ds(HALO + j * part, part)], kv_got.at[g, at, j])

        for at in range(2):
            for p in range(len(pieces)):
                wait_part(at, pieces[p][0])

                @pl.when(c < nc - 1)
                def _():
                    halo_copy(g, at, p).start()

        for at in range(2):
            for j in range(nh):
                wait_part(at, j)

    def turn(g, first, last):
        for i in range(first, last):
            turned[i] = keys_in[g][i * BLK : (i + 1) * BLK, :].T

    def finish_kv(g):
        turn(g, MAXDOC - 1, MAXDOC - 1 + blocks)

        @pl.when(c > 0)
        def _():
            for at in range(2):
                for p in range(len(pieces)):
                    halo_copy(g, at, p).wait_recv()

        @pl.when(c == 0)
        def _():
            for ref in (keys_in[g], values_in[g]):
                ref[0:HALO, :] = jnp.zeros((HALO, HD), ref.dtype)

        turn(g, 0, MAXDOC - 1)
        v_work[...] = values_in[g][...].reshape(v_work.shape)

    causal = lax.broadcasted_iota(jnp.int32, (BLK, BLK), 1) <= lax.broadcasted_iota(
        jnp.int32, (BLK, BLK), 0
    )

    def attend(g, k, slot):
        block = slot_block[slot]
        count = slot_count[slot]
        queries = q_work[block]
        keys = jnp.concatenate([turned[block + i] for i in range(MAXDOC)], axis=1)
        values = jnp.concatenate([v_work[block + i] for i in range(MAXDOC)], axis=0)
        scores = jnp.dot(queries, keys, preferred_element_type=jnp.float32)
        parts = [scores[:, i * BLK : (i + 1) * BLK] for i in range(MAXDOC)]
        for i in range(MAXDOC - 1):
            inside = jnp.full((BLK, BLK), count - (MAXDOC - 1 - i), jnp.int32) > 0
            parts[i] = jnp.where(inside, parts[i], -jnp.inf)
        parts[-1] = jnp.where(causal, parts[-1], -jnp.inf)
        top = jnp.max(functools.reduce(jnp.maximum, parts), axis=1, keepdims=True)
        parts = [jnp.exp2((x - top) * factor) for x in parts]
        total = jnp.sum(functools.reduce(jnp.add, parts), axis=1, keepdims=True)
        weights = jnp.concatenate([x.astype(jnp.bfloat16) for x in parts], axis=1)
        mixed = jnp.dot(weights, values, preferred_element_type=jnp.float32) / total
        out[k, slot] = mixed.astype(out.dtype)

    def columns(k):
        return pl.ds(aligned(k * HD), HD)

    def send_out(k, d):
        t = lax.rem(c + d, nc)
        pltpu.make_async_remote_copy(
            src_ref=out.at[k, pl.ds(t * cap, cap)],
            dst_ref=got_ref.at[pl.ds(c * cap, cap), :, columns(k)],
            send_sem=out_sent.at[k],
            recv_sem=out_got.at[k],
            device_id=(t, h),
            device_id_type=MESH,
        ).start()

    def own_copy(k):
        mine = pl.ds(c * cap, cap)
        return pltpu.make_async_copy(
            out.at[k, mine], got_ref.at[mine, :, columns(k)], own_done.at[k]
        )

    def head_step(g, k):
        for j in range(nh):
            wait_on(q_in.at[k, pl.ds(j * part, part)], q_got.at[k, j])
        q_work[...] = q_in[k].reshape(q_work.shape)

        def target(d, carry):
            t = lax.rem(c + d, nc)
            for r in range(cap):
                attend(g, k, t * cap + r)

            @pl.when(d > 1)
            def _():
                send_out(k, d - 1)

            return carry

        lax.fori_loop(1, nc + 1, target, 0)
        own_copy(k).start()

    gather_kv(0)
    for g in range(kv_heads):
        finish_kv(g)

        def one(k, carry, g=g):
            head_step(g, k)
            return carry

        lax.fori_loop(g * group, g * group + 1, one, 0)
        if g + 1 < kv_heads:
            gather_kv(g + 1)
        lax.fori_loop(g * group + 1, (g + 1) * group, one, 0)

    for g in range(kv_heads):
        for at in range(2):
            for d in range(1, nh):
                wait_on(keys_in[g].at[my_kv_rows], kv_sent.at[g, at, d])

            @pl.when(c < nc - 1)
            def _():
                for p in range(len(pieces)):
                    halo_copy(g, at, p).wait_send()

    def drain(k, carry):
        for d in range(1, nh):
            wait_on(q_in.at[k, my_rows], q_sent.at[k, d])
        own_copy(k).wait()
        wait_on(out.at[k, pl.ds(0, (nc - 1) * cap)], out_sent.at[k])
        wait_on(got_ref.at[pl.ds(0, (nc - 1) * cap), :, columns(k)], out_got.at[k])
        return carry

    lax.fori_loop(0, heads, drain, 0)


def fused(slot_block, slot_count, query, key, value):
    nc, nh = lax.axis_size("ctx"), lax.axis_size("head")
    part = query.shape[0]
    rows = nh * part
    heads = query.shape[1] // nh // HD
    kv_heads = key.shape[1] // nh // HD
    cap = -(-(rows // BLK) // nc)
    slots = nc * cap
    window = HALO + rows
    dma = pltpu.SemaphoreType.DMA
    return pl.pallas_call(
        functools.partial(fused_kernel, kv_heads, cap),
        out_shape=jax.ShapeDtypeStruct((slots, BLK, heads * HD), query.dtype),
        in_specs=[pl.BlockSpec(memory_space=pltpu.SMEM)] * 2
        + [pl.BlockSpec(memory_space=pl.ANY)] * 3,
        out_specs=pl.BlockSpec(memory_space=pl.ANY),
        scratch_shapes=[pltpu.VMEM((window, HD), query.dtype)] * (2 * kv_heads)
        + [
            pltpu.VMEM((heads, rows, HD), query.dtype),
            pltpu.VMEM((rows // BLK, BLK, HD), query.dtype),
            pltpu.VMEM((window // BLK, HD, BLK), query.dtype),
            pltpu.VMEM((window // BLK, BLK, HD), query.dtype),
            pltpu.VMEM((heads, slots, BLK, HD), query.dtype),
            dma((heads, nh)),
            dma((heads, nh)),
            dma((kv_heads, 2, nh)),
            dma((kv_heads, 2, nh)),
            dma((kv_heads, 2, nh)),
            dma((kv_heads, 2, nh)),
            dma((heads,)),
            dma((heads,)),
            dma((heads,)),
        ],
        compiler_params=pltpu.CompilerParams(collective_id=0, has_side_effects=True),
        name="fused",
    )(slot_block, slot_count, query, key, value)


def prepare_kernel(blocks, cap, doc_ref, plan_ref, slot_block, slot_count, mine):
    c, nc = lax.axis_index("ctx"), lax.axis_size("ctx")

    def table(k, carry):
        found = [jnp.int32(0)] * cap
        seen = jnp.int32(0)
        for i in range(blocks):
            p = plan_ref[k * blocks + i]
            hit = lax.div(p, blocks) == c
            for r in range(cap):
                found[r] = jnp.where(hit & (seen == r), lax.rem(p, blocks), found[r])
            seen = seen + jnp.where(hit, 1, 0)
        for r in range(cap):
            at = c * blocks + found[r]
            document = doc_ref[at]
            count = jnp.int32(1)
            for t in range(1, MAXDOC):
                same = doc_ref[jnp.maximum(at - t, 0)] == document
                count = count + jnp.where((at >= t) & same, 1, 0)
            slot_block[k * cap + r] = found[r]
            slot_count[k * cap + r] = count
        return carry

    lax.fori_loop(0, nc, table, 0)

    sources = [lax.div(plan_ref[c * blocks + i], blocks) for i in range(blocks)]
    for i in range(blocks):
        rank = jnp.int32(0)
        for before in range(i):
            rank = rank + jnp.where(sources[before] == sources[i], 1, 0)
        mine[i] = sources[i] * cap + jnp.minimum(rank, cap - 1)


def prepare(doc_ids, plan, blocks, cap):
    slots = lax.axis_size("ctx") * cap
    sizes = (slots, slots, blocks)
    return pl.pallas_call(
        functools.partial(prepare_kernel, blocks, cap),
        out_shape=[jax.ShapeDtypeStruct((n,), jnp.int32) for n in sizes],
        in_specs=[pl.BlockSpec(memory_space=pltpu.SMEM)] * 2,
        out_specs=[pl.BlockSpec(memory_space=pltpu.SMEM)] * 3,
        name="prepare",
    )(doc_ids, plan)


def place_kernel(mine_ref, got_ref, o_ref, stage, in_sems, out_sems):
    blocks = o_ref.shape[0] // BLK
    incoming = []
    for i in range(blocks):
        copy = pltpu.make_async_copy(got_ref.at[mine_ref[i]], stage.at[i], in_sems.at[i])
        copy.start()
        incoming.append(copy)
    outgoing = []
    for i in range(blocks):
        incoming[i].wait()
        copy = pltpu.make_async_copy(
            stage.at[i], o_ref.at[pl.ds(i * BLK, BLK)], out_sems.at[i]
        )
        copy.start()
        outgoing.append(copy)
    for copy in outgoing:
        copy.wait()


def place(mine, got):
    blocks = mine.shape[0]
    width = got.shape[2]
    return pl.pallas_call(
        place_kernel,
        out_shape=jax.ShapeDtypeStruct((blocks * BLK, width), got.dtype),
        in_specs=[
            pl.BlockSpec(memory_space=pltpu.SMEM),
            pl.BlockSpec(memory_space=pl.ANY),
        ],
        out_specs=pl.BlockSpec(memory_space=pl.ANY),
        scratch_shapes=[
            pltpu.VMEM((blocks, BLK, width), got.dtype),
            pltpu.SemaphoreType.DMA((blocks,)),
            pltpu.SemaphoreType.DMA((blocks,)),
        ],
        name="place",
    )(mine, got)


def shards(query, key, value, doc_ids, plan):
    blocks = lax.axis_size("head") * query.shape[0] // BLK
    cap = -(-blocks // lax.axis_size("ctx"))
    slot_block, slot_count, mine = prepare(doc_ids, plan, blocks, cap)
    return place(mine, fused(slot_block, slot_count, query, key, value))


def solution(mesh):
    return jax.shard_map(
        shards,
        mesh=mesh,
        in_specs=(
            P(("ctx", "head"), None),
            P(("ctx", "head"), None),
            P(("ctx", "head"), None),
            P(),
            P(),
        ),
        out_specs=P("ctx", "head"),
        check_vma=False,
    )
```

```python
import functools
import math

import jax
import jax.numpy as jnp
from jax import lax
from jax.experimental import pallas as pl
from jax.experimental.pallas import tpu as pltpu
from jax.sharding import PartitionSpec as P

HD = 128
BLK = 128
MAXDOC = 8
HALO = (MAXDOC - 1) * BLK
EARLY = 3
MESH = pl.DeviceIdType.MESH


def aligned(x):
    return pl.multiple_of(x, BLK)


def fused_kernel(
    kv_heads, cap, doc_ref, plan_ref, q_ref, k_ref, v_ref, got_ref, mine_ref, slot_block, slot_count, *rest
):
    keys_in = rest[:kv_heads]
    values_in = rest[kv_heads : 2 * kv_heads]
    q_in, q_work, turned, v_work, out = rest[2 * kv_heads : 2 * kv_heads + 5]
    sems = rest[2 * kv_heads + 5 :]
    q_sent, q_got, kv_sent, kv_got, halo_sent, halo_got, out_sent, out_got, own_done = sems
    c, h = lax.axis_index("ctx"), lax.axis_index("head")
    nc, nh = lax.axis_size("ctx"), lax.axis_size("head")
    part = q_ref.shape[0]
    rows = nh * part
    blocks = rows // BLK
    heads = q_in.shape[0]
    group = heads // kv_heads
    factor = math.log2(math.e) / math.sqrt(HD)

    barrier = pltpu.get_barrier_semaphore()
    for d in range(1, nh):
        pl.semaphore_signal(
            barrier, inc=1, device_id=(c, lax.rem(h + d, nh)), device_id_type=MESH
        )
    for d in range(1, nc):
        pl.semaphore_signal(
            barrier, inc=1, device_id=(lax.rem(c + d, nc), h), device_id_type=MESH
        )
    pl.semaphore_wait(barrier, nh + nc - 2)

    my_rows = pl.ds(aligned(h * part), part)
    my_kv_rows = pl.ds(aligned(HALO + h * part), part)

    def send_kv(g):
        for at, (src, dst) in enumerate(((k_ref, keys_in[g]), (v_ref, values_in[g]))):
            for d in range(1, nh):
                t = lax.rem(h + d, nh)
                pltpu.make_async_remote_copy(
                    src_ref=src.at[:, pl.ds(aligned((t * kv_heads + g) * HD), HD)],
                    dst_ref=dst.at[my_kv_rows],
                    send_sem=kv_sent.at[g, at, d],
                    recv_sem=kv_got.at[g, at, h],
                    device_id=(c, t),
                    device_id_type=MESH,
                ).start()
            pltpu.make_async_copy(
                src.at[:, pl.ds(aligned((h * kv_heads + g) * HD), HD)],
                dst.at[my_kv_rows],
                kv_got.at[g, at, h],
            ).start()

    def send_q(k):
        for d in range(1, nh):
            t = lax.rem(h + d, nh)
            pltpu.make_async_remote_copy(
                src_ref=q_ref.at[:, pl.ds(aligned((t * heads + k) * HD), HD)],
                dst_ref=q_in.at[k, my_rows],
                send_sem=q_sent.at[k, d],
                recv_sem=q_got.at[k, h],
                device_id=(c, t),
                device_id_type=MESH,
            ).start()
        pltpu.make_async_copy(
            q_ref.at[:, pl.ds(aligned((h * heads + k) * HD), HD)],
            q_in.at[k, my_rows],
            q_got.at[k, h],
        ).start()

    def wait_on(ref, sem):
        pltpu.make_async_copy(ref, ref, sem).wait()

    def send_q_loop(k, carry):
        send_q(k)
        return carry

    send_kv(0)
    sent = 0
    for g in range(1, kv_heads):
        upto = (g - 1) * group + EARLY
        lax.fori_loop(sent, upto, send_q_loop, 0)
        send_kv(g)
        sent = upto
    lax.fori_loop(sent, heads, send_q_loop, 0)

    def table(k, carry):
        found = [jnp.int32(0)] * cap
        seen = jnp.int32(0)
        for i in range(blocks):
            p = plan_ref[k * blocks + i]
            hit = lax.div(p, blocks) == c
            for r in range(cap):
                found[r] = jnp.where(hit & (seen == r), lax.rem(p, blocks), found[r])
            seen = seen + jnp.where(hit, 1, 0)
        for r in range(cap):
            at = c * blocks + found[r]
            document = doc_ref[at]
            count = jnp.int32(1)
            for t in range(1, MAXDOC):
                same = doc_ref[jnp.maximum(at - t, 0)] == document
                count = count + jnp.where((at >= t) & same, 1, 0)
            slot_block[k * cap + r] = found[r]
            slot_count[k * cap + r] = count
        return carry

    lax.fori_loop(0, nc, table, 0)

    sources = [lax.div(plan_ref[c * blocks + i], blocks) for i in range(blocks)]
    for i in range(blocks):
        rank = jnp.int32(0)
        for before in range(i):
            rank = rank + jnp.where(sources[before] == sources[i], 1, 0)
        mine_ref[i] = sources[i] * cap + jnp.minimum(rank, cap - 1)

    pieces = []
    for j in range(nh - 1, -1, -1):
        low, high = max(rows - HALO, j * part), (j + 1) * part
        if low < high:
            pieces.append((j, low, high - low))

    def halo_copy(g, at, p):
        ref = (keys_in[g], values_in[g])[at]
        _, low, size = pieces[p]
        return pltpu.make_async_remote_copy(
            src_ref=ref.at[pl.ds(HALO + low, size)],
            dst_ref=ref.at[pl.ds(HALO + low - rows, size)],
            send_sem=halo_sent.at[g, at, p],
            recv_sem=halo_got.at[g, at, p],
            device_id=(jnp.minimum(c + 1, nc - 1), h),
            device_id_type=MESH,
        )

    def gather_kv(g):
        waited = set()

        def wait_part(at, j):
            if (at, j) not in waited:
                waited.add((at, j))
                ref = (keys_in[g], values_in[g])[at]
                wait_on(ref.at[pl.ds(HALO + j * part, part)], kv_got.at[g, at, j])

        for at in range(2):
            for p in range(len(pieces)):
                wait_part(at, pieces[p][0])

                @pl.when(c < nc - 1)
                def _():
                    halo_copy(g, at, p).start()

        for at in range(2):
            for j in range(nh):
                wait_part(at, j)

    def turn(g, first, last):
        for i in range(first, last):
            turned[i] = keys_in[g][i * BLK : (i + 1) * BLK, :].T

    def finish_kv(g):
        turn(g, MAXDOC - 1, MAXDOC - 1 + blocks)

        @pl.when(c > 0)
        def _():
            for at in range(2):
                for p in range(len(pieces)):
                    halo_copy(g, at, p).wait_recv()

        @pl.when(c == 0)
        def _():
            for ref in (keys_in[g], values_in[g]):
                ref[0:HALO, :] = jnp.zeros((HALO, HD), ref.dtype)

        turn(g, 0, MAXDOC - 1)
        v_work[...] = values_in[g][...].reshape(v_work.shape)

    causal = lax.broadcasted_iota(jnp.int32, (BLK, BLK), 1) <= lax.broadcasted_iota(
        jnp.int32, (BLK, BLK), 0
    )

    def attend(g, k, slot):
        block = slot_block[slot]
        count = slot_count[slot]
        queries = q_work[block]
        keys = jnp.concatenate([turned[block + i] for i in range(MAXDOC)], axis=1)
        values = jnp.concatenate([v_work[block + i] for i in range(MAXDOC)], axis=0)
        scores = jnp.dot(queries, keys, preferred_element_type=jnp.float32)
        parts = [scores[:, i * BLK : (i + 1) * BLK] for i in range(MAXDOC)]
        for i in range(MAXDOC - 1):
            inside = jnp.full((BLK, BLK), count - (MAXDOC - 1 - i), jnp.int32) > 0
            parts[i] = jnp.where(inside, parts[i], -jnp.inf)
        parts[-1] = jnp.where(causal, parts[-1], -jnp.inf)
        top = jnp.max(functools.reduce(jnp.maximum, parts), axis=1, keepdims=True)
        parts = [jnp.exp2((x - top) * factor) for x in parts]
        total = jnp.sum(functools.reduce(jnp.add, parts), axis=1, keepdims=True)
        weights = jnp.concatenate([x.astype(jnp.bfloat16) for x in parts], axis=1)
        mixed = jnp.dot(weights, values, preferred_element_type=jnp.float32) / total
        out[k, slot] = mixed.astype(out.dtype)

    def columns(k):
        return pl.ds(aligned(k * HD), HD)

    def send_out(k, d):
        t = lax.rem(c + d, nc)
        pltpu.make_async_remote_copy(
            src_ref=out.at[k, pl.ds(t * cap, cap)],
            dst_ref=got_ref.at[pl.ds(c * cap, cap), :, columns(k)],
            send_sem=out_sent.at[k],
            recv_sem=out_got.at[k],
            device_id=(t, h),
            device_id_type=MESH,
        ).start()

    def own_copy(k):
        mine = pl.ds(c * cap, cap)
        return pltpu.make_async_copy(
            out.at[k, mine], got_ref.at[mine, :, columns(k)], own_done.at[k]
        )

    def head_step(g, k):
        for j in range(nh):
            wait_on(q_in.at[k, pl.ds(j * part, part)], q_got.at[k, j])
        q_work[...] = q_in[k].reshape(q_work.shape)

        def target(d, carry):
            t = lax.rem(c + d, nc)
            for r in range(cap):
                attend(g, k, t * cap + r)

            @pl.when(d > 1)
            def _():
                send_out(k, d - 1)

            return carry

        lax.fori_loop(1, nc + 1, target, 0)
        own_copy(k).start()

    gather_kv(0)
    for g in range(kv_heads):
        finish_kv(g)

        def one(k, carry, g=g):
            head_step(g, k)
            return carry

        lax.fori_loop(g * group, g * group + EARLY, one, 0)
        if g + 1 < kv_heads:
            gather_kv(g + 1)
        lax.fori_loop(g * group + EARLY, (g + 1) * group, one, 0)

    for g in range(kv_heads):
        for at in range(2):
            for d in range(1, nh):
                wait_on(keys_in[g].at[my_kv_rows], kv_sent.at[g, at, d])

            @pl.when(c < nc - 1)
            def _():
                for p in range(len(pieces)):
                    halo_copy(g, at, p).wait_send()

    def drain(k, carry):
        for d in range(1, nh):
            wait_on(q_in.at[k, my_rows], q_sent.at[k, d])
        own_copy(k).wait()
        wait_on(out.at[k, pl.ds(0, (nc - 1) * cap)], out_sent.at[k])
        wait_on(got_ref.at[pl.ds(0, (nc - 1) * cap), :, columns(k)], out_got.at[k])
        return carry

    lax.fori_loop(0, heads, drain, 0)


def fused(doc_ids, plan, query, key, value):
    nc, nh = lax.axis_size("ctx"), lax.axis_size("head")
    part = query.shape[0]
    rows = nh * part
    heads = query.shape[1] // nh // HD
    kv_heads = key.shape[1] // nh // HD
    cap = -(-(rows // BLK) // nc)
    slots = nc * cap
    window = HALO + rows
    dma = pltpu.SemaphoreType.DMA
    elements = (2 * kv_heads + 2) * window + (heads + 1) * rows + heads * slots * BLK
    held = 2 * elements * HD
    return pl.pallas_call(
        functools.partial(fused_kernel, kv_heads, cap),
        out_shape=[
            jax.ShapeDtypeStruct((slots, BLK, heads * HD), query.dtype),
            jax.ShapeDtypeStruct((rows // BLK,), jnp.int32),
        ],
        in_specs=[pl.BlockSpec(memory_space=pltpu.SMEM)] * 2
        + [pl.BlockSpec(memory_space=pltpu.HBM)] * 3,
        out_specs=[
            pl.BlockSpec(memory_space=pl.ANY),
            pl.BlockSpec(memory_space=pltpu.SMEM),
        ],
        scratch_shapes=[pltpu.SMEM((slots,), jnp.int32)] * 2
        + [pltpu.VMEM((window, HD), query.dtype)] * (2 * kv_heads)
        + [
            pltpu.VMEM((heads, rows, HD), query.dtype),
            pltpu.VMEM((rows // BLK, BLK, HD), query.dtype),
            pltpu.VMEM((window // BLK, HD, BLK), query.dtype),
            pltpu.VMEM((window // BLK, BLK, HD), query.dtype),
            pltpu.VMEM((heads, slots, BLK, HD), query.dtype),
            dma((heads, nh)),
            dma((heads, nh)),
            dma((kv_heads, 2, nh)),
            dma((kv_heads, 2, nh)),
            dma((kv_heads, 2, nh)),
            dma((kv_heads, 2, nh)),
            dma((heads,)),
            dma((heads,)),
            dma((heads,)),
        ],
        compiler_params=pltpu.CompilerParams(
            collective_id=0, has_side_effects=True, vmem_limit_bytes=held + (6 << 20)
        ),
        name="fused",
    )(doc_ids, plan, query, key, value)


def place_kernel(mine_ref, got_ref, o_ref, sems):
    copies = []
    for i in range(o_ref.shape[0] // BLK):
        copy = pltpu.make_async_copy(
            got_ref.at[mine_ref[i]], o_ref.at[pl.ds(i * BLK, BLK)], sems.at[i]
        )
        copy.start()
        copies.append(copy)
    for copy in copies:
        copy.wait()


def place(mine, got):
    blocks = mine.shape[0]
    width = got.shape[2]
    return pl.pallas_call(
        place_kernel,
        out_shape=jax.ShapeDtypeStruct((blocks * BLK, width), got.dtype),
        in_specs=[
            pl.BlockSpec(memory_space=pltpu.SMEM),
            pl.BlockSpec(memory_space=pl.ANY),
        ],
        out_specs=pl.BlockSpec(memory_space=pl.ANY),
        scratch_shapes=[pltpu.SemaphoreType.DMA((blocks,))],
        compiler_params=pltpu.CompilerParams(vmem_limit_bytes=1 << 20),
        name="place",
    )(mine, got)


def shards(query, key, value, doc_ids, plan):
    operands = [
        pltpu.with_memory_space_constraint(x, pltpu.HBM)
        for x in (doc_ids, plan, query, key, value)
    ]
    got, mine = fused(*operands)
    return place(mine, got)


def solution(mesh):
    return jax.shard_map(
        shards,
        mesh=mesh,
        in_specs=(
            P(("ctx", "head"), None),
            P(("ctx", "head"), None),
            P(("ctx", "head"), None),
            P(),
            P(),
        ),
        out_specs=P("ctx", "head"),
        check_vma=False,
    )
```

```python
import functools
import math

import jax
import jax.numpy as jnp
from jax import lax
from jax.experimental import pallas as pl
from jax.experimental.pallas import tpu as pltpu
from jax.sharding import PartitionSpec as P

HD = 128
BLK = 128
MAXDOC = 8
HALO = (MAXDOC - 1) * BLK
MESH = pl.DeviceIdType.MESH


def collected_at(n):
    return (n - 1) * 3 // 2


def aligned(x):
    return pl.multiple_of(x, BLK)


def fused_kernel(
    kv_heads,
    cap,
    doc_ref,
    plan_ref,
    q_ref,
    k_ref,
    v_ref,
    got_ref,
    mine_ref,
    slot_block,
    slot_count,
    keys_in,
    values_in,
    stage,
    q_in,
    q_work,
    turned,
    v_work,
    out,
    q_sent,
    q_got,
    kv_sent,
    kv_passed,
    kv_got,
    halo_sent,
    halo_passed,
    halo_got,
    stage_sent,
    stage_got,
    out_sent,
    out_got,
    own_sent,
    own_got,
    ready,
):
    c, h = lax.axis_index("ctx"), lax.axis_index("head")
    nc, nh = lax.axis_size("ctx"), lax.axis_size("head")
    pairs = nh // 2
    pair, side = lax.div(h, 2), lax.rem(h, 2)
    partner = h + 1 - 2 * side
    part = q_ref.shape[0]
    rows = nh * part
    blocks = rows // BLK
    heads = q_in.shape[0]
    shared = 2 * kv_heads
    half = heads // shared
    factor = math.log2(math.e) / math.sqrt(HD)
    sources = (k_ref, v_ref)
    windows = (keys_in, values_in)

    barrier = pltpu.get_barrier_semaphore()
    for d in range(1, nh):
        pl.semaphore_signal(
            barrier, inc=1, device_id=(c, lax.rem(h + d, nh)), device_id_type=MESH
        )

    @pl.when(c > 0)
    def _():
        pl.semaphore_signal(barrier, inc=1, device_id=(c - 1, h), device_id_type=MESH)

    @pl.when(c < nc - 1)
    def _():
        pl.semaphore_signal(barrier, inc=1, device_id=(c + 1, h), device_id_type=MESH)

    near = jnp.where(c > 0, 1, 0) + jnp.where(c < nc - 1, 1, 0)
    pl.semaphore_wait(barrier, nh - 1 + near)

    my_rows = pl.ds(aligned(h * part), part)

    def rows_of(j):
        return pl.ds(aligned(HALO + j * part), part)

    def wait_on(ref, sem):
        pltpu.make_async_copy(ref, ref, sem).wait()

    def send_kv(n):
        for at in range(2):
            dst = windows[at].at[n, rows_of(h)]
            for d in range(pairs):
                other = lax.rem(pair + d, pairs)
                pltpu.make_async_remote_copy(
                    src_ref=sources[at].at[:, pl.ds(aligned((other * shared + n) * HD), HD)],
                    dst_ref=dst,
                    send_sem=kv_sent.at[n, at, d],
                    recv_sem=kv_got.at[n, at, h],
                    device_id=(c, 2 * other + side if d else partner),
                    device_id_type=MESH,
                ).start()
            pltpu.make_async_copy(
                sources[at].at[:, pl.ds(aligned((pair * shared + n) * HD), HD)],
                dst,
                kv_got.at[n, at, h],
            ).start()

    def q_columns(k, t):
        pair_of, side_of = lax.div(t, 2), lax.rem(t, 2)
        n, i = lax.div(k, half), lax.rem(k, half)
        first = 2 * pair_of * heads + n * 2 * half + side_of * half + i
        return pl.ds(aligned(first * HD), HD)

    def send_q(k):
        for d in range(1, nh):
            t = lax.rem(h + d, nh)
            pltpu.make_async_remote_copy(
                src_ref=q_ref.at[:, q_columns(k, t)],
                dst_ref=q_in.at[k, my_rows],
                send_sem=q_sent.at[k, d],
                recv_sem=q_got.at[k, h],
                device_id=(c, t),
                device_id_type=MESH,
            ).start()
        pltpu.make_async_copy(
            q_ref.at[:, q_columns(k, h)], q_in.at[k, my_rows], q_got.at[k, h]
        ).start()

    def send_loop(k, carry):
        send_q(k)
        for n in range(1, shared):

            @pl.when(k == collected_at(n))
            def _(n=n):
                send_kv(n)

        return carry

    send_kv(0)
    lax.fori_loop(0, heads, send_loop, 0)

    step, d = 0, 1
    while d < nc:
        below, above = c >= d, c + d < nc
        for there, other, mark in ((below, c - d, 1), (above, c + d, 0)):

            @pl.when(there)
            def _(other=other, mark=mark, step=step):
                pl.semaphore_signal(
                    ready.at[step, mark], inc=1, device_id=(other, h), device_id_type=MESH
                )

        for there, mark in ((below, 0), (above, 1)):

            @pl.when(there)
            def _(mark=mark, step=step):
                pl.semaphore_wait(ready.at[step, mark], 1)

        step, d = step + 1, 2 * d

    def table(k, carry):
        found = [jnp.int32(0)] * cap
        seen = jnp.int32(0)
        for i in range(blocks):
            p = plan_ref[k * blocks + i]
            hit = lax.div(p, blocks) == c
            for r in range(cap):
                found[r] = jnp.where(hit & (seen == r), lax.rem(p, blocks), found[r])
            seen = seen + jnp.where(hit, 1, 0)
        for r in range(cap):
            at = c * blocks + found[r]
            document = doc_ref[at]
            count = jnp.int32(1)
            for t in range(1, MAXDOC):
                same = doc_ref[jnp.maximum(at - t, 0)] == document
                count = count + jnp.where((at >= t) & same, 1, 0)
            slot_block[k * cap + r] = found[r]
            slot_count[k * cap + r] = count
        return carry

    lax.fori_loop(0, nc, table, 0)

    origins = [lax.div(plan_ref[c * blocks + i], blocks) for i in range(blocks)]
    for i in range(blocks):
        rank = jnp.int32(0)
        for before in range(i):
            rank = rank + jnp.where(origins[before] == origins[i], 1, 0)
        mine_ref[i] = origins[i] * cap + jnp.minimum(rank, cap - 1)

    pieces = []
    for j in range(nh - 1, -1, -1):
        low, high = max(rows - HALO, j * part), (j + 1) * part
        if low < high:
            pieces.append((j, low, high - low))

    odd = lax.rem(c, 2) == 1
    has_next = c < nc - 1

    def for_pieces(mine, act):
        for j, low, size in pieces:

            @pl.when((side == j % 2) if mine else (side != j % 2))
            def _(j=j, low=low, size=size):
                act(j, low, size)

    def halo_copy(n, at, j, low, size):
        ref = windows[at]
        return pltpu.make_async_remote_copy(
            src_ref=ref.at[n, pl.ds(HALO + low, size)],
            dst_ref=ref.at[n, pl.ds(HALO + low - rows, size)],
            send_sem=halo_sent.at[n, at, j],
            recv_sem=halo_got.at[n, at, j],
            device_id=(jnp.minimum(c + 1, nc - 1), h),
            device_id_type=MESH,
        )

    def detour_copy(n, j, low, size):
        return pltpu.make_async_remote_copy(
            src_ref=values_in.at[n, pl.ds(HALO + low, size)],
            dst_ref=stage.at[n, pl.ds(HALO + low - rows, size)],
            send_sem=halo_sent.at[n, 1, j],
            recv_sem=stage_got.at[n, j],
            device_id=(jnp.maximum(c - 1, 0), h),
            device_id_type=MESH,
        )

    def relay_copy(n, j, low, size):
        held = pl.ds(HALO + low - rows, size)
        return pltpu.make_async_remote_copy(
            src_ref=stage.at[n, held],
            dst_ref=values_in.at[n, held],
            send_sem=stage_sent.at[n, j],
            recv_sem=halo_got.at[n, 1, j],
            device_id=(jnp.minimum(c + 2, nc - 1), h),
            device_id_type=MESH,
        )

    def pass_halo_copy(n, at, j, low, size):
        ref = windows[at].at[n, pl.ds(HALO + low - rows, size)]
        return pltpu.make_async_remote_copy(
            src_ref=ref,
            dst_ref=ref,
            send_sem=halo_passed.at[n, at, j],
            recv_sem=halo_got.at[n, at, j],
            device_id=(c, partner),
            device_id_type=MESH,
        )

    def pass_kv_copy(n, at, d):
        j = 2 * lax.rem(pair + d, pairs) + side
        ref = windows[at].at[n, rows_of(j)]
        return pltpu.make_async_remote_copy(
            src_ref=ref,
            dst_ref=ref,
            send_sem=kv_passed.at[n, at, d],
            recv_sem=kv_got.at[n, at, j],
            device_id=(c, partner),
            device_id_type=MESH,
        )

    def collect(n):
        for at in range(2):
            for d in range(pairs):
                j = 2 * lax.rem(pair + d, pairs) + side
                wait_on(windows[at].at[n, rows_of(j)], kv_got.at[n, at, j])
                if d:
                    pass_kv_copy(n, at, d).start()

            straight = has_next
            if at and n:
                straight = has_next & jnp.logical_not(odd)

                @pl.when(has_next & odd)
                def _():
                    for_pieces(True, lambda *p: detour_copy(n, *p).start())

            @pl.when(straight)
            def _(at=at):
                for_pieces(True, lambda *p: halo_copy(n, at, *p).start())

    relays = jnp.logical_not(odd) & (c + 2 < nc)

    def relay(n):
        @pl.when(relays)
        def _():
            def act(*p):
                relay_copy(n, *p).start()

            def arrived(j, low, size):
                wait_on(stage.at[n, pl.ds(HALO + low - rows, size)], stage_got.at[n, j])
                act(j, low, size)

            for_pieces(True, arrived)

    def pass_halo(n):
        @pl.when(c > 0)
        def _():
            for at in range(2):

                def act(j, low, size, at=at):
                    held = windows[at].at[n, pl.ds(HALO + low - rows, size)]
                    wait_on(held, halo_got.at[n, at, j])
                    pass_halo_copy(n, at, j, low, size).start()

                for_pieces(True, act)

    def turn(n, first, last):
        for i in range(first, last):
            turned[i] = keys_in[n, i * BLK : (i + 1) * BLK, :].T
            v_work[i] = values_in[n, i * BLK : (i + 1) * BLK, :]

    def turn_rows(n):
        for at in range(2):
            for other in range(pairs):
                j = 2 * other + 1 - side
                wait_on(windows[at].at[n, rows_of(j)], kv_got.at[n, at, j])
        turn(n, MAXDOC - 1, MAXDOC - 1 + blocks)

    def turn_halo(n):
        @pl.when(c > 0)
        def _():
            for at in range(2):

                def act(j, low, size, at=at):
                    held = windows[at].at[n, pl.ds(HALO + low - rows, size)]
                    wait_on(held, halo_got.at[n, at, j])

                for_pieces(False, act)
            turn(n, 0, MAXDOC - 1)

        @pl.when(c == 0)
        def _():
            for ref in (turned, v_work):
                ref[0 : MAXDOC - 1] = jnp.zeros((MAXDOC - 1,) + ref.shape[1:], ref.dtype)

    causal = lax.broadcasted_iota(jnp.int32, (BLK, BLK), 1) <= lax.broadcasted_iota(
        jnp.int32, (BLK, BLK), 0
    )

    def attend(k, slot):
        block = slot_block[slot]
        count = slot_count[slot]
        queries = q_work[block]
        keys = jnp.concatenate([turned[block + i] for i in range(MAXDOC)], axis=1)
        values = jnp.concatenate([v_work[block + i] for i in range(MAXDOC)], axis=0)
        scores = jnp.dot(queries, keys, preferred_element_type=jnp.float32)
        parts = [scores[:, i * BLK : (i + 1) * BLK] for i in range(MAXDOC)]
        for i in range(MAXDOC - 1):
            inside = jnp.full((BLK, BLK), count - (MAXDOC - 1 - i), jnp.int32) > 0
            parts[i] = jnp.where(inside, parts[i], -jnp.inf)
        parts[-1] = jnp.where(causal, parts[-1], -jnp.inf)
        top = jnp.max(functools.reduce(jnp.maximum, parts), axis=1, keepdims=True)
        parts = [jnp.exp2((x - top) * factor) for x in parts]
        total = jnp.sum(functools.reduce(jnp.add, parts), axis=1, keepdims=True)
        weights = jnp.concatenate([x.astype(jnp.bfloat16) for x in parts], axis=1)
        mixed = jnp.dot(weights, values, preferred_element_type=jnp.float32) / total
        out[k, slot] = mixed.astype(out.dtype)

    def owner(k):
        return 2 * pair + lax.div(lax.div(k, half), kv_heads)

    def column(k):
        n, i = lax.div(k, half), lax.rem(k, half)
        return lax.rem(n, kv_heads) * 2 * half + side * half + i

    def columns(col):
        return pl.ds(aligned(col * HD), HD)

    def send_out(k, d):
        t = lax.rem(c + d, nc)
        col = column(k)
        pltpu.make_async_remote_copy(
            src_ref=out.at[k, pl.ds(t * cap, cap)],
            dst_ref=got_ref.at[pl.ds(c * cap, cap), :, columns(col)],
            send_sem=out_sent.at[k],
            recv_sem=out_got.at[col],
            device_id=(t, owner(k)),
            device_id_type=MESH,
        ).start()

    own_slots = pl.ds(c * cap, cap)

    def send_own(k):
        col = column(k)
        src = out.at[k, own_slots]
        dst = got_ref.at[own_slots, :, columns(col)]

        @pl.when(owner(k) == h)
        def _():
            pltpu.make_async_copy(src, dst, own_got.at[col]).start()

        @pl.when(owner(k) != h)
        def _():
            pltpu.make_async_remote_copy(
                src_ref=src,
                dst_ref=dst,
                send_sem=own_sent.at[k],
                recv_sem=own_got.at[col],
                device_id=(c, partner),
                device_id_type=MESH,
            ).start()

    def head_step(k):
        for j in range(nh):
            wait_on(q_in.at[k, pl.ds(j * part, part)], q_got.at[k, j])
        q_work[...] = q_in[k].reshape(q_work.shape)

        def target(d, carry):
            t = lax.rem(c + d, nc)
            for r in range(cap):
                attend(k, t * cap + r)
                if r == 0:

                    @pl.when(d > 1)
                    def _():
                        send_out(k, d - 1)

            return carry

        lax.fori_loop(1, nc + 1, target, 0)
        send_own(k)

    collect(0)
    turn_rows(0)
    pass_halo(0)
    turn_halo(0)

    def one(k, carry):
        n, i = lax.div(k, half), lax.rem(k, half)

        @pl.when((i == 0) & (n > 0))
        def _():
            turn_rows(n)
            turn_halo(n)

        head_step(k)
        for later in range(1, shared):
            for wait, act in ((2, pass_halo), (1, relay), (0, collect)):

                @pl.when(k == collected_at(later) + wait)
                def _(later=later, act=act):
                    act(later)

        return carry

    lax.fori_loop(0, heads, one, 0)

    def settle_kv(n, first):
        for at in range(2):
            for d in range(pairs):
                wait_on(windows[at].at[n, rows_of(h)], kv_sent.at[n, at, d])
                if d:
                    pass_kv_copy(n, at, d).wait_send()

            @pl.when(has_next)
            def _(at=at):
                for_pieces(True, lambda *p: halo_copy(n, at, *p).wait_send())

            @pl.when(c > 0)
            def _(at=at):
                for_pieces(True, lambda *p: pass_halo_copy(n, at, *p).wait_send())

        if not first:

            @pl.when(relays)
            def _():
                for_pieces(True, lambda *p: relay_copy(n, *p).wait_send())

    settle_kv(0, True)

    def settle(n, carry):
        settle_kv(n, False)
        return carry

    lax.fori_loop(1, shared, settle, 0)

    def drain(k, carry):
        for d in range(1, nh):
            wait_on(q_in.at[k, my_rows], q_sent.at[k, d])

        @pl.when(owner(k) != h)
        def _():
            wait_on(out.at[k, own_slots], own_sent.at[k])

        wait_on(out.at[k, pl.ds(0, (nc - 1) * cap)], out_sent.at[k])
        wait_on(got_ref.at[own_slots, :, columns(k)], own_got.at[k])
        wait_on(got_ref.at[pl.ds(0, (nc - 1) * cap), :, columns(k)], out_got.at[k])
        return carry

    lax.fori_loop(0, heads, drain, 0)


def fused(doc_ids, plan, query, key, value):
    nc, nh = lax.axis_size("ctx"), lax.axis_size("head")
    part = query.shape[0]
    rows = nh * part
    blocks = rows // BLK
    heads = query.shape[1] // nh // HD
    kv_heads = key.shape[1] // nh // HD
    shared = 2 * kv_heads
    cap = -(-blocks // nc)
    slots = nc * cap
    window = HALO + rows
    dma = pltpu.SemaphoreType.DMA
    buffers = [
        (shared, window, HD),
        (shared, window, HD),
        (shared, HALO, HD),
        (heads, rows, HD),
        (blocks, BLK, HD),
        (window // BLK, HD, BLK),
        (window // BLK, BLK, HD),
        (heads, slots, BLK, HD),
    ]
    held = 2 * sum(math.prod(shape) for shape in buffers)
    return pl.pallas_call(
        functools.partial(fused_kernel, kv_heads, cap),
        out_shape=[
            jax.ShapeDtypeStruct((slots, BLK, heads * HD), query.dtype),
            jax.ShapeDtypeStruct((blocks,), jnp.int32),
        ],
        in_specs=[pl.BlockSpec(memory_space=pltpu.SMEM)] * 2
        + [pl.BlockSpec(memory_space=pltpu.HBM)] * 3,
        out_specs=[
            pl.BlockSpec(memory_space=pl.ANY),
            pl.BlockSpec(memory_space=pltpu.SMEM),
        ],
        scratch_shapes=[pltpu.SMEM((slots,), jnp.int32)] * 2
        + [pltpu.VMEM(shape, query.dtype) for shape in buffers]
        + [dma((heads, nh))] * 2
        + [dma((shared, 2, nh))] * 6
        + [dma((shared, nh))] * 2
        + [dma((heads,))] * 4
        + [pltpu.SemaphoreType.REGULAR((nc.bit_length(), 2))],
        compiler_params=pltpu.CompilerParams(
            collective_id=0, has_side_effects=True, vmem_limit_bytes=held + (6 << 20)
        ),
        name="fused",
    )(doc_ids, plan, query, key, value)


def place_kernel(mine_ref, got_ref, o_ref, sems):
    copies = []
    for i in range(o_ref.shape[0] // BLK):
        copy = pltpu.make_async_copy(
            got_ref.at[mine_ref[i]], o_ref.at[pl.ds(i * BLK, BLK)], sems.at[i]
        )
        copy.start()
        copies.append(copy)
    for copy in copies:
        copy.wait()


def place(mine, got):
    blocks = mine.shape[0]
    width = got.shape[2]
    return pl.pallas_call(
        place_kernel,
        out_shape=jax.ShapeDtypeStruct((blocks * BLK, width), got.dtype),
        in_specs=[
            pl.BlockSpec(memory_space=pltpu.SMEM),
            pl.BlockSpec(memory_space=pl.ANY),
        ],
        out_specs=pl.BlockSpec(memory_space=pl.ANY),
        scratch_shapes=[pltpu.SemaphoreType.DMA((blocks,))],
        compiler_params=pltpu.CompilerParams(vmem_limit_bytes=1 << 20),
        name="place",
    )(mine, got)


def shards(query, key, value, doc_ids, plan):
    operands = [
        pltpu.with_memory_space_constraint(x, pltpu.HBM)
        for x in (doc_ids, plan, query, key, value)
    ]
    got, mine = fused(*operands)
    return place(mine, got)


def solution(mesh):
    return jax.shard_map(
        shards,
        mesh=mesh,
        in_specs=(
            P(("ctx", "head"), None),
            P(("ctx", "head"), None),
            P(("ctx", "head"), None),
            P(),
            P(),
        ),
        out_specs=P("ctx", "head"),
        check_vma=False,
    )
```

```python
import functools
import math

import jax
import jax.numpy as jnp
from jax import lax
from jax.experimental import pallas as pl
from jax.experimental.pallas import tpu as pltpu
from jax.sharding import PartitionSpec as P

HD = 128
BLK = 128
MAXDOC = 8
HALO = (MAXDOC - 1) * BLK
MESH = pl.DeviceIdType.MESH


def collected_at(n):
    return (n - 1) * 3 // 2


def aligned(x):
    return pl.multiple_of(x, BLK)


def fused_kernel(
    kv_heads,
    cap,
    doc_ref,
    plan_ref,
    q_ref,
    k_ref,
    v_ref,
    got_ref,
    mine_ref,
    slot_block,
    slot_count,
    keys_in,
    values_in,
    stage,
    q_in,
    q_work,
    turned,
    v_work,
    out,
    q_sent,
    q_got,
    kv_sent,
    kv_passed,
    kv_got,
    halo_sent,
    halo_passed,
    halo_got,
    stage_sent,
    stage_got,
    out_sent,
    out_got,
    own_sent,
    own_got,
    ready,
):
    c, h = lax.axis_index("ctx"), lax.axis_index("head")
    nc, nh = lax.axis_size("ctx"), lax.axis_size("head")
    pairs = nh // 2
    pair, side = lax.div(h, 2), lax.rem(h, 2)
    partner = h + 1 - 2 * side
    part = q_ref.shape[0]
    rows = nh * part
    blocks = rows // BLK
    heads = q_in.shape[0]
    shared = 2 * kv_heads
    half = heads // shared
    factor = math.log2(math.e) / math.sqrt(HD)
    sources = (k_ref, v_ref)
    windows = (keys_in, values_in)

    barrier = pltpu.get_barrier_semaphore()
    for d in range(1, nh):
        pl.semaphore_signal(
            barrier, inc=1, device_id=(c, lax.rem(h + d, nh)), device_id_type=MESH
        )

    @pl.when(c > 0)
    def _():
        pl.semaphore_signal(barrier, inc=1, device_id=(c - 1, h), device_id_type=MESH)

    @pl.when(c < nc - 1)
    def _():
        pl.semaphore_signal(barrier, inc=1, device_id=(c + 1, h), device_id_type=MESH)

    near = jnp.where(c > 0, 1, 0) + jnp.where(c < nc - 1, 1, 0)
    pl.semaphore_wait(barrier, nh - 1 + near)

    my_rows = pl.ds(aligned(h * part), part)

    def rows_of(j):
        return pl.ds(aligned(HALO + j * part), part)

    def wait_on(ref, sem):
        pltpu.make_async_copy(ref, ref, sem).wait()

    def send_kv(n):
        for at in range(2):
            dst = windows[at].at[n, rows_of(h)]
            for d in range(pairs):
                other = lax.rem(pair + d, pairs)
                pltpu.make_async_remote_copy(
                    src_ref=sources[at].at[:, pl.ds(aligned((other * shared + n) * HD), HD)],
                    dst_ref=dst,
                    send_sem=kv_sent.at[n, at, d],
                    recv_sem=kv_got.at[n, at, h],
                    device_id=(c, 2 * other + side if d else partner),
                    device_id_type=MESH,
                ).start()
            pltpu.make_async_copy(
                sources[at].at[:, pl.ds(aligned((pair * shared + n) * HD), HD)],
                dst,
                kv_got.at[n, at, h],
            ).start()

    def q_columns(k, t):
        pair_of, side_of = lax.div(t, 2), lax.rem(t, 2)
        n, i = lax.div(k, half), lax.rem(k, half)
        first = 2 * pair_of * heads + n * 2 * half + side_of * half + i
        return pl.ds(aligned(first * HD), HD)

    def send_q(k):
        for d in range(1, nh):
            t = lax.rem(h + d, nh)
            pltpu.make_async_remote_copy(
                src_ref=q_ref.at[:, q_columns(k, t)],
                dst_ref=q_in.at[k, my_rows],
                send_sem=q_sent.at[k, d],
                recv_sem=q_got.at[k, h],
                device_id=(c, t),
                device_id_type=MESH,
            ).start()
        pltpu.make_async_copy(
            q_ref.at[:, q_columns(k, h)], q_in.at[k, my_rows], q_got.at[k, h]
        ).start()

    def send_loop(k, carry):
        send_q(k)
        for n in range(1, shared):

            @pl.when(k == collected_at(n))
            def _(n=n):
                send_kv(n)

        return carry

    send_kv(0)
    lax.fori_loop(0, heads, send_loop, 0)

    step, d = 0, 1
    while d < nc:
        below, above = c >= d, c + d < nc
        for there, other, mark in ((below, c - d, 1), (above, c + d, 0)):

            @pl.when(there)
            def _(other=other, mark=mark, step=step):
                pl.semaphore_signal(
                    ready.at[step, mark], inc=1, device_id=(other, h), device_id_type=MESH
                )

        for there, mark in ((below, 0), (above, 1)):

            @pl.when(there)
            def _(mark=mark, step=step):
                pl.semaphore_wait(ready.at[step, mark], 1)

        step, d = step + 1, 2 * d

    def table(k, carry):
        found = [jnp.int32(0)] * cap
        seen = jnp.int32(0)
        for i in range(blocks):
            p = plan_ref[k * blocks + i]
            hit = lax.div(p, blocks) == c
            for r in range(cap):
                found[r] = jnp.where(hit & (seen == r), lax.rem(p, blocks), found[r])
            seen = seen + jnp.where(hit, 1, 0)
        for r in range(cap):
            at = c * blocks + found[r]
            document = doc_ref[at]
            count = jnp.int32(1)
            for t in range(1, MAXDOC):
                same = doc_ref[jnp.maximum(at - t, 0)] == document
                count = count + jnp.where((at >= t) & same, 1, 0)
            slot_block[k * cap + r] = found[r]
            slot_count[k * cap + r] = count
        return carry

    lax.fori_loop(0, nc, table, 0)

    origins = [lax.div(plan_ref[c * blocks + i], blocks) for i in range(blocks)]
    for i in range(blocks):
        rank = jnp.int32(0)
        for before in range(i):
            rank = rank + jnp.where(origins[before] == origins[i], 1, 0)
        mine_ref[i] = origins[i] * cap + jnp.minimum(rank, cap - 1)

    pieces = []
    for j in range(nh - 1, -1, -1):
        low, high = max(rows - HALO, j * part), (j + 1) * part
        if low < high:
            pieces.append((j, low, high - low))

    odd = lax.rem(c, 2) == 1
    has_next = c < nc - 1

    def for_pieces(mine, act):
        for j, low, size in pieces:

            @pl.when((side == j % 2) if mine else (side != j % 2))
            def _(j=j, low=low, size=size):
                act(j, low, size)

    def halo_copy(n, at, j, low, size):
        ref = windows[at]
        return pltpu.make_async_remote_copy(
            src_ref=ref.at[n, pl.ds(HALO + low, size)],
            dst_ref=ref.at[n, pl.ds(HALO + low - rows, size)],
            send_sem=halo_sent.at[n, at, j],
            recv_sem=halo_got.at[n, at, j],
            device_id=(jnp.minimum(c + 1, nc - 1), h),
            device_id_type=MESH,
        )

    def detour_copy(n, j, low, size):
        return pltpu.make_async_remote_copy(
            src_ref=values_in.at[n, pl.ds(HALO + low, size)],
            dst_ref=stage.at[n, pl.ds(HALO + low - rows, size)],
            send_sem=halo_sent.at[n, 1, j],
            recv_sem=stage_got.at[n, j],
            device_id=(jnp.maximum(c - 1, 0), h),
            device_id_type=MESH,
        )

    def relay_copy(n, j, low, size):
        held = pl.ds(HALO + low - rows, size)
        return pltpu.make_async_remote_copy(
            src_ref=stage.at[n, held],
            dst_ref=values_in.at[n, held],
            send_sem=stage_sent.at[n, j],
            recv_sem=halo_got.at[n, 1, j],
            device_id=(jnp.minimum(c + 2, nc - 1), h),
            device_id_type=MESH,
        )

    def pass_halo_copy(n, at, j, low, size):
        ref = windows[at].at[n, pl.ds(HALO + low - rows, size)]
        return pltpu.make_async_remote_copy(
            src_ref=ref,
            dst_ref=ref,
            send_sem=halo_passed.at[n, at, j],
            recv_sem=halo_got.at[n, at, j],
            device_id=(c, partner),
            device_id_type=MESH,
        )

    def pass_kv_copy(n, at, d):
        j = 2 * lax.rem(pair + d, pairs) + side
        ref = windows[at].at[n, rows_of(j)]
        return pltpu.make_async_remote_copy(
            src_ref=ref,
            dst_ref=ref,
            send_sem=kv_passed.at[n, at, d],
            recv_sem=kv_got.at[n, at, j],
            device_id=(c, partner),
            device_id_type=MESH,
        )

    def collect(n):
        for at in range(2):
            for d in range(pairs):
                j = 2 * lax.rem(pair + d, pairs) + side
                wait_on(windows[at].at[n, rows_of(j)], kv_got.at[n, at, j])
                if d:
                    pass_kv_copy(n, at, d).start()

            straight = has_next
            if at and n:
                straight = has_next & jnp.logical_not(odd)

                @pl.when(has_next & odd)
                def _():
                    for_pieces(True, lambda *p: detour_copy(n, *p).start())

            @pl.when(straight)
            def _(at=at):
                for_pieces(True, lambda *p: halo_copy(n, at, *p).start())

    relays = jnp.logical_not(odd) & (c + 2 < nc)

    def relay(n):
        @pl.when(relays)
        def _():
            def act(*p):
                relay_copy(n, *p).start()

            def arrived(j, low, size):
                wait_on(stage.at[n, pl.ds(HALO + low - rows, size)], stage_got.at[n, j])
                act(j, low, size)

            for_pieces(True, arrived)

    def pass_halo(n):
        @pl.when(c > 0)
        def _():
            for at in range(2):

                def act(j, low, size, at=at):
                    held = windows[at].at[n, pl.ds(HALO + low - rows, size)]
                    wait_on(held, halo_got.at[n, at, j])
                    pass_halo_copy(n, at, j, low, size).start()

                for_pieces(True, act)

    def turn(n, first, last):
        for i in range(first, last):
            turned[i] = keys_in[n, i * BLK : (i + 1) * BLK, :].T
            v_work[i] = values_in[n, i * BLK : (i + 1) * BLK, :]

    def turn_rows(n):
        for at in range(2):
            for other in range(pairs):
                j = 2 * other + 1 - side
                wait_on(windows[at].at[n, rows_of(j)], kv_got.at[n, at, j])
        turn(n, MAXDOC - 1, MAXDOC - 1 + blocks)

    def turn_halo(n):
        @pl.when(c > 0)
        def _():
            for at in range(2):

                def act(j, low, size, at=at):
                    held = windows[at].at[n, pl.ds(HALO + low - rows, size)]
                    wait_on(held, halo_got.at[n, at, j])

                for_pieces(False, act)
            turn(n, 0, MAXDOC - 1)

        @pl.when(c == 0)
        def _():
            for ref in (turned, v_work):
                ref[0 : MAXDOC - 1] = jnp.zeros((MAXDOC - 1,) + ref.shape[1:], ref.dtype)

    causal = lax.broadcasted_iota(jnp.int32, (BLK, BLK), 1) <= lax.broadcasted_iota(
        jnp.int32, (BLK, BLK), 0
    )

    def attend(k, slot):
        block = slot_block[slot]
        count = slot_count[slot]
        queries = q_work[block]
        keys = jnp.concatenate([turned[block + i] for i in range(MAXDOC)], axis=1)
        values = jnp.concatenate([v_work[block + i] for i in range(MAXDOC)], axis=0)
        scores = jnp.dot(queries, keys, preferred_element_type=jnp.float32)
        parts = [scores[:, i * BLK : (i + 1) * BLK] for i in range(MAXDOC)]
        for i in range(MAXDOC - 1):
            inside = jnp.full((BLK, BLK), count - (MAXDOC - 1 - i), jnp.int32) > 0
            parts[i] = jnp.where(inside, parts[i], -jnp.inf)
        parts[-1] = jnp.where(causal, parts[-1], -jnp.inf)
        top = jnp.max(functools.reduce(jnp.maximum, parts), axis=1, keepdims=True)
        parts = [jnp.exp2((x - top) * factor) for x in parts]
        total = jnp.sum(functools.reduce(jnp.add, parts), axis=1, keepdims=True)
        weights = jnp.concatenate([x.astype(jnp.bfloat16) for x in parts], axis=1)
        mixed = jnp.dot(weights, values, preferred_element_type=jnp.float32) / total
        out[k, slot] = mixed.astype(out.dtype)

    def owner(k):
        return 2 * pair + lax.div(lax.div(k, half), kv_heads)

    def column(k):
        n, i = lax.div(k, half), lax.rem(k, half)
        return lax.rem(n, kv_heads) * 2 * half + side * half + i

    def columns(col):
        return pl.ds(aligned(col * HD), HD)

    def target_of(s):
        away = nc // 2 + (1 - 2 * lax.rem(s, 2)) * lax.div(s + 1, 2)
        return lax.rem(c + away, nc)

    def send_out(k, s):
        t = target_of(s)
        col = column(k)
        pltpu.make_async_remote_copy(
            src_ref=out.at[k, pl.ds(t * cap, cap)],
            dst_ref=got_ref.at[pl.ds(c * cap, cap), :, columns(col)],
            send_sem=out_sent.at[k],
            recv_sem=out_got.at[col],
            device_id=(t, owner(k)),
            device_id_type=MESH,
        ).start()

    own_slots = pl.ds(c * cap, cap)

    def send_own(k):
        col = column(k)
        src = out.at[k, own_slots]
        dst = got_ref.at[own_slots, :, columns(col)]

        @pl.when(owner(k) == h)
        def _():
            pltpu.make_async_copy(src, dst, own_got.at[col]).start()

        @pl.when(owner(k) != h)
        def _():
            pltpu.make_async_remote_copy(
                src_ref=src,
                dst_ref=dst,
                send_sem=own_sent.at[k],
                recv_sem=own_got.at[col],
                device_id=(c, partner),
                device_id_type=MESH,
            ).start()

    def head_step(k):
        for j in range(nh):
            wait_on(q_in.at[k, pl.ds(j * part, part)], q_got.at[k, j])
        q_work[...] = q_in[k].reshape(q_work.shape)

        def target(s, carry):
            t = target_of(s)
            for r in range(cap):
                attend(k, t * cap + r)
                if r == 0:

                    @pl.when(s > 0)
                    def _():
                        send_out(k, s - 1)

            return carry

        lax.fori_loop(0, nc, target, 0)
        send_own(k)

    collect(0)
    turn_rows(0)
    pass_halo(0)
    turn_halo(0)

    def one(k, carry):
        n, i = lax.div(k, half), lax.rem(k, half)

        @pl.when((i == 0) & (n > 0))
        def _():
            turn_rows(n)
            turn_halo(n)

        head_step(k)
        for later in range(1, shared):
            for wait, act in ((2, pass_halo), (1, relay), (0, collect)):

                @pl.when(k == collected_at(later) + wait)
                def _(later=later, act=act):
                    act(later)

        return carry

    lax.fori_loop(0, heads, one, 0)

    def settle_kv(n, first):
        for at in range(2):
            for d in range(pairs):
                wait_on(windows[at].at[n, rows_of(h)], kv_sent.at[n, at, d])
                if d:
                    pass_kv_copy(n, at, d).wait_send()

            @pl.when(has_next)
            def _(at=at):
                for_pieces(True, lambda *p: halo_copy(n, at, *p).wait_send())

            @pl.when(c > 0)
            def _(at=at):
                for_pieces(True, lambda *p: pass_halo_copy(n, at, *p).wait_send())

        if not first:

            @pl.when(relays)
            def _():
                for_pieces(True, lambda *p: relay_copy(n, *p).wait_send())

    settle_kv(0, True)

    def settle(n, carry):
        settle_kv(n, False)
        return carry

    lax.fori_loop(1, shared, settle, 0)

    def drain(k, carry):
        for d in range(1, nh):
            wait_on(q_in.at[k, my_rows], q_sent.at[k, d])

        @pl.when(owner(k) != h)
        def _():
            wait_on(out.at[k, own_slots], own_sent.at[k])

        wait_on(out.at[k, pl.ds(0, (nc - 1) * cap)], out_sent.at[k])
        wait_on(got_ref.at[own_slots, :, columns(k)], own_got.at[k])
        wait_on(got_ref.at[pl.ds(0, (nc - 1) * cap), :, columns(k)], out_got.at[k])
        return carry

    lax.fori_loop(0, heads, drain, 0)


def fused(doc_ids, plan, query, key, value):
    nc, nh = lax.axis_size("ctx"), lax.axis_size("head")
    part = query.shape[0]
    rows = nh * part
    blocks = rows // BLK
    heads = query.shape[1] // nh // HD
    kv_heads = key.shape[1] // nh // HD
    shared = 2 * kv_heads
    cap = -(-blocks // nc)
    slots = nc * cap
    window = HALO + rows
    dma = pltpu.SemaphoreType.DMA
    buffers = [
        (shared, window, HD),
        (shared, window, HD),
        (shared, HALO, HD),
        (heads, rows, HD),
        (blocks, BLK, HD),
        (window // BLK, HD, BLK),
        (window // BLK, BLK, HD),
        (heads, slots, BLK, HD),
    ]
    held = 2 * sum(math.prod(shape) for shape in buffers)
    return pl.pallas_call(
        functools.partial(fused_kernel, kv_heads, cap),
        out_shape=[
            jax.ShapeDtypeStruct((slots, BLK, heads * HD), query.dtype),
            jax.ShapeDtypeStruct((blocks,), jnp.int32),
        ],
        in_specs=[pl.BlockSpec(memory_space=pltpu.SMEM)] * 2
        + [pl.BlockSpec(memory_space=pltpu.HBM)] * 3,
        out_specs=[
            pl.BlockSpec(memory_space=pl.ANY),
            pl.BlockSpec(memory_space=pltpu.SMEM),
        ],
        scratch_shapes=[pltpu.SMEM((slots,), jnp.int32)] * 2
        + [pltpu.VMEM(shape, query.dtype) for shape in buffers]
        + [dma((heads, nh))] * 2
        + [dma((shared, 2, nh))] * 6
        + [dma((shared, nh))] * 2
        + [dma((heads,))] * 4
        + [pltpu.SemaphoreType.REGULAR((nc.bit_length(), 2))],
        compiler_params=pltpu.CompilerParams(
            collective_id=0, has_side_effects=True, vmem_limit_bytes=held + (6 << 20)
        ),
        name="fused",
    )(doc_ids, plan, query, key, value)


def place_kernel(mine_ref, got_ref, o_ref, sems):
    copies = []
    for i in range(o_ref.shape[0] // BLK):
        copy = pltpu.make_async_copy(
            got_ref.at[mine_ref[i]], o_ref.at[pl.ds(i * BLK, BLK)], sems.at[i]
        )
        copy.start()
        copies.append(copy)
    for copy in copies:
        copy.wait()


def place(mine, got):
    blocks = mine.shape[0]
    width = got.shape[2]
    return pl.pallas_call(
        place_kernel,
        out_shape=jax.ShapeDtypeStruct((blocks * BLK, width), got.dtype),
        in_specs=[
            pl.BlockSpec(memory_space=pltpu.SMEM),
            pl.BlockSpec(memory_space=pl.ANY),
        ],
        out_specs=pl.BlockSpec(memory_space=pl.ANY),
        scratch_shapes=[pltpu.SemaphoreType.DMA((blocks,))],
        compiler_params=pltpu.CompilerParams(vmem_limit_bytes=1 << 20),
        name="place",
    )(mine, got)


def shards(query, key, value, doc_ids, plan):
    operands = [
        pltpu.with_memory_space_constraint(x, pltpu.HBM)
        for x in (doc_ids, plan, query, key, value)
    ]
    got, mine = fused(*operands)
    return place(mine, got)


def solution(mesh):
    return jax.shard_map(
        shards,
        mesh=mesh,
        in_specs=(
            P(("ctx", "head"), None),
            P(("ctx", "head"), None),
            P(("ctx", "head"), None),
            P(),
            P(),
        ),
        out_specs=P("ctx", "head"),
        check_vma=False,
    )
```

```python
import functools
import math

import jax
import jax.numpy as jnp
from jax import lax
from jax.experimental import pallas as pl
from jax.experimental.pallas import tpu as pltpu
from jax.sharding import PartitionSpec as P

HD = 128
BLK = 128
MAXDOC = 8
HALO = (MAXDOC - 1) * BLK
AHEAD = 8
DIRECT = 3
MESH = pl.DeviceIdType.MESH


def aligned(x):
    return pl.multiple_of(x, BLK)


def fused_kernel(
    kv_heads,
    cap,
    doc_ref,
    plan_ref,
    q_ref,
    k_ref,
    v_ref,
    got_ref,
    mine_ref,
    slot_block,
    slot_count,
    keys_in,
    values_in,
    via,
    stage,
    q_in,
    q_work,
    turned,
    v_work,
    out,
    q_sent,
    q_got,
    kv_sent,
    kv_passed,
    kv_got,
    halo_sent,
    halo_passed,
    halo_got,
    away_sent,
    via_got,
    via_sent,
    stage_got,
    stage_sent,
    out_sent,
    out_got,
    own_sent,
    own_got,
    ready,
):
    c, h = lax.axis_index("ctx"), lax.axis_index("head")
    nc, nh = lax.axis_size("ctx"), lax.axis_size("head")
    pairs = nh // 2
    pair, side = lax.div(h, 2), lax.rem(h, 2)
    partner = h + 1 - 2 * side
    part = q_ref.shape[0]
    rows = nh * part
    blocks = rows // BLK
    heads = q_in.shape[0]
    shared = 2 * kv_heads
    half = heads // shared
    factor = math.log2(math.e) / math.sqrt(HD)
    sources = (k_ref, v_ref)
    windows = (keys_in, values_in)

    barrier = pltpu.get_barrier_semaphore()
    for d in range(1, nh):
        pl.semaphore_signal(
            barrier, inc=1, device_id=(c, lax.rem(h + d, nh)), device_id_type=MESH
        )

    @pl.when(c > 0)
    def _():
        pl.semaphore_signal(barrier, inc=1, device_id=(c - 1, h), device_id_type=MESH)

    @pl.when(c < nc - 1)
    def _():
        pl.semaphore_signal(barrier, inc=1, device_id=(c + 1, h), device_id_type=MESH)

    near = jnp.where(c > 0, 1, 0) + jnp.where(c < nc - 1, 1, 0)
    pl.semaphore_wait(barrier, nh - 1 + near)

    my_rows = pl.ds(aligned(h * part), part)

    def rows_of(j):
        return pl.ds(aligned(HALO + j * part), part)

    def wait_on(ref, sem):
        pltpu.make_async_copy(ref, ref, sem).wait()

    def send_kv(n):
        for at in range(2):
            dst = windows[at].at[n, rows_of(h)]
            for d in range(pairs):
                other = lax.rem(pair + d, pairs)
                pltpu.make_async_remote_copy(
                    src_ref=sources[at].at[:, pl.ds(aligned((other * shared + n) * HD), HD)],
                    dst_ref=dst,
                    send_sem=kv_sent.at[n, at, d],
                    recv_sem=kv_got.at[n, at, h],
                    device_id=(c, 2 * other + side if d else partner),
                    device_id_type=MESH,
                ).start()
            pltpu.make_async_copy(
                sources[at].at[:, pl.ds(aligned((pair * shared + n) * HD), HD)],
                dst,
                kv_got.at[n, at, h],
            ).start()

    def q_columns(k, t):
        pair_of, side_of = lax.div(t, 2), lax.rem(t, 2)
        n, i = lax.div(k, half), lax.rem(k, half)
        first = 2 * pair_of * heads + n * 2 * half + side_of * half + i
        return pl.ds(aligned(first * HD), HD)

    def send_q(k):
        for d in range(1, nh):
            t = lax.rem(h + d, nh)
            pltpu.make_async_remote_copy(
                src_ref=q_ref.at[:, q_columns(k, t)],
                dst_ref=q_in.at[k, my_rows],
                send_sem=q_sent.at[k, d],
                recv_sem=q_got.at[k, h],
                device_id=(c, t),
                device_id_type=MESH,
            ).start()
        pltpu.make_async_copy(
            q_ref.at[:, q_columns(k, h)], q_in.at[k, my_rows], q_got.at[k, h]
        ).start()

    pieces = []
    for j in range(nh - 1, -1, -1):
        low, high = max(rows - HALO, j * part), (j + 1) * part
        if low < high:
            pieces.append((j, low, high - low))

    odd = lax.rem(c, 2) == 1
    has_next = c < nc - 1
    following = jnp.minimum(c + 1, nc - 1)
    relays = jnp.logical_not(odd) & (c + 2 < nc)

    def for_pieces(mine, act):
        for j, low, size in pieces:

            @pl.when((side == j % 2) if mine else (side != j % 2))
            def _(j=j, low=low, size=size):
                act(j, low, size)

    def for_own_pieces(act):
        for j, low, size in pieces:

            @pl.when(h == j)
            def _(j=j, low=low, size=size):
                act(j, low, size)

    def for_other_pairs(act):
        for at in range(2):
            for d in range(1, pairs):
                act(at, d)

    def halo_rows(low, size):
        return pl.ds(HALO + low - rows, size)

    def rows_in(at, n, d, j, low, size):
        other = lax.rem(pair + d, pairs)
        return sources[at].at[
            pl.ds(low - j * part, size), pl.ds(aligned((other * shared + n) * HD), HD)
        ]

    def halo_copy(n, at, j, low, size, src):
        return pltpu.make_async_remote_copy(
            src_ref=src,
            dst_ref=windows[at].at[n, halo_rows(low, size)],
            send_sem=halo_sent.at[n, at, j],
            recv_sem=halo_got.at[n, at, j],
            device_id=(following, h),
            device_id_type=MESH,
        )

    def place_of(n, d):
        return (d - 1) * (shared - DIRECT) + n - DIRECT

    def away_copy(n, at, d, j, low, size, back):
        q = place_of(n, d)
        return pltpu.make_async_remote_copy(
            src_ref=rows_in(at, n, d, j, low, size),
            dst_ref=(via if back else stage).at[at, q, halo_rows(low, size)],
            send_sem=away_sent.at[at, q, j],
            recv_sem=(via_got if back else stage_got).at[at, q, j],
            device_id=(jnp.maximum(c - 1, 0) if back else following, h),
            device_id_type=MESH,
        )

    def lead(n, who):
        @pl.when(has_next & who)
        def _():
            def own_pair(j, low, size):
                for at in range(2):
                    src = rows_in(at, n, 0, j, low, size)
                    halo_copy(n, at, j, low, size, src).start()

            for_own_pieces(own_pair)

        if n >= DIRECT:
            for back, turn_of in ((True, odd), (False, jnp.logical_not(odd))):

                @pl.when(has_next & who & turn_of)
                def _(back=back):
                    for_own_pieces(
                        lambda *p: for_other_pairs(
                            lambda at, d: away_copy(n, at, d, *p, back).start()
                        )
                    )

    def send_kv_after(k):
        for n in range(1, shared):
            if k == 2 * n - 2:
                send_kv(n)

    always = c >= 0
    lead(0, always)
    send_kv(0)
    for k in range(min(AHEAD, heads)):
        send_q(k)
        send_kv_after(k)
        if k == 0:
            for n in range(1, shared):
                lead(n, always if n == 1 else odd)

    step, d = 0, 1
    while d < nc:
        below, above = c >= d, c + d < nc
        for there, other, mark in ((below, c - d, 1), (above, c + d, 0)):

            @pl.when(there)
            def _(other=other, mark=mark, step=step):
                pl.semaphore_signal(
                    ready.at[step, mark], inc=1, device_id=(other, h), device_id_type=MESH
                )

        for there, mark in ((below, 0), (above, 1)):

            @pl.when(there)
            def _(mark=mark, step=step):
                pl.semaphore_wait(ready.at[step, mark], 1)

        step, d = step + 1, 2 * d

    def table(k, carry):
        found = [jnp.int32(0)] * cap
        seen = jnp.int32(0)
        for i in range(blocks):
            p = plan_ref[k * blocks + i]
            hit = lax.div(p, blocks) == c
            for r in range(cap):
                found[r] = jnp.where(hit & (seen == r), lax.rem(p, blocks), found[r])
            seen = seen + jnp.where(hit, 1, 0)
        for r in range(cap):
            at = c * blocks + found[r]
            document = doc_ref[at]
            count = jnp.int32(1)
            for t in range(1, MAXDOC):
                same = doc_ref[jnp.maximum(at - t, 0)] == document
                count = count + jnp.where((at >= t) & same, 1, 0)
            slot_block[k * cap + r] = found[r]
            slot_count[k * cap + r] = count
        return carry

    lax.fori_loop(0, nc, table, 0)

    origins = [lax.div(plan_ref[c * blocks + i], blocks) for i in range(blocks)]
    for i in range(blocks):
        rank = jnp.int32(0)
        for before in range(i):
            rank = rank + jnp.where(origins[before] == origins[i], 1, 0)
        mine_ref[i] = origins[i] * cap + jnp.minimum(rank, cap - 1)

    def pass_halo_copy(n, at, j, low, size):
        ref = windows[at].at[n, halo_rows(low, size)]
        return pltpu.make_async_remote_copy(
            src_ref=ref,
            dst_ref=ref,
            send_sem=halo_passed.at[n, at, j],
            recv_sem=halo_got.at[n, at, j],
            device_id=(c, partner),
            device_id_type=MESH,
        )

    def pass_kv_copy(n, at, d):
        j = 2 * lax.rem(pair + d, pairs) + side
        ref = windows[at].at[n, rows_of(j)]
        return pltpu.make_async_remote_copy(
            src_ref=ref,
            dst_ref=ref,
            send_sem=kv_passed.at[n, at, d],
            recv_sem=kv_got.at[n, at, j],
            device_id=(c, partner),
            device_id_type=MESH,
        )

    def collect(n):
        for at in range(2):
            for d in range(pairs):
                j = 2 * lax.rem(pair + d, pairs) + side
                wait_on(windows[at].at[n, rows_of(j)], kv_got.at[n, at, j])
                if d:
                    pass_kv_copy(n, at, d).start()
            if n >= DIRECT:
                continue

            def act(j, low, size, at=at):
                @pl.when((h != j) & (odd if n and at else False))
                def _():
                    detour_copy(n, j, low, size).start()

                @pl.when((h != j) & jnp.logical_not(odd if n and at else False))
                def _():
                    src = windows[at].at[n, pl.ds(HALO + low, size)]
                    halo_copy(n, at, j, low, size, src).start()

            @pl.when(has_next)
            def _(act=act):
                for_pieces(True, act)

    def detour_copy(n, j, low, size):
        return pltpu.make_async_remote_copy(
            src_ref=values_in.at[n, pl.ds(HALO + low, size)],
            dst_ref=via.at[1, n - 1, halo_rows(low, size)],
            send_sem=halo_sent.at[n, 1, j],
            recv_sem=via_got.at[1, n - 1, j],
            device_id=(jnp.maximum(c - 1, 0), h),
            device_id_type=MESH,
        )

    def detour_on_copy(n, j, low, size):
        held = halo_rows(low, size)
        return pltpu.make_async_remote_copy(
            src_ref=via.at[1, n - 1, held],
            dst_ref=values_in.at[n, held],
            send_sem=via_sent.at[1, n - 1, j],
            recv_sem=halo_got.at[n, 1, j],
            device_id=(jnp.minimum(c + 2, nc - 1), h),
            device_id_type=MESH,
        )

    def detour_on(n):
        @pl.when(relays)
        def _():
            def act(j, low, size):
                @pl.when(h != j)
                def _():
                    wait_on(via.at[1, n - 1, halo_rows(low, size)], via_got.at[1, n - 1, j])
                    detour_on_copy(n, j, low, size).start()

            for_pieces(True, act)

    def relay_copy(n, at, d, j, low, size):
        q = place_of(n, d)
        held = halo_rows(low, size)
        return pltpu.make_async_remote_copy(
            src_ref=via.at[at, q, held],
            dst_ref=stage.at[at, q, held],
            send_sem=via_sent.at[at, q, j],
            recv_sem=stage_got.at[at, q, j],
            device_id=(jnp.minimum(c + 2, nc - 1), h),
            device_id_type=MESH,
        )

    def relay(n):
        @pl.when(relays)
        def _():
            def act(j, low, size):
                def one_of(at, d):
                    q = place_of(n, d)
                    wait_on(via.at[at, q, halo_rows(low, size)], via_got.at[at, q, j])
                    relay_copy(n, at, d, j, low, size).start()

                for_other_pairs(one_of)

            for_own_pieces(act)

    def spread_copy(n, at, d, j, low, size):
        q = place_of(n, d)
        held = halo_rows(low, size)
        return pltpu.make_async_remote_copy(
            src_ref=stage.at[at, q, held],
            dst_ref=windows[at].at[n, held],
            send_sem=stage_sent.at[at, q, j],
            recv_sem=halo_got.at[n, at, j],
            device_id=(c, 2 * lax.rem(pair + d, pairs) + side),
            device_id_type=MESH,
        )

    def spread(n):
        @pl.when(c > 0)
        def _():
            def act(j, low, size):
                def one_of(at, d):
                    q = place_of(n, d)
                    wait_on(stage.at[at, q, halo_rows(low, size)], stage_got.at[at, q, j])
                    spread_copy(n, at, d, j, low, size).start()

                for_other_pairs(one_of)

            for_own_pieces(act)

    def pass_halo(n):
        @pl.when(c > 0)
        def _():
            for at in range(2):

                def act(j, low, size, at=at):
                    held = windows[at].at[n, halo_rows(low, size)]
                    wait_on(held, halo_got.at[n, at, j])
                    pass_halo_copy(n, at, j, low, size).start()

                for_pieces(True, act)

    def turn(n, first, last):
        for i in range(first, last):
            turned[i] = keys_in[n, i * BLK : (i + 1) * BLK, :].T
            v_work[i] = values_in[n, i * BLK : (i + 1) * BLK, :]

    def turn_rows(n):
        for at in range(2):
            for other in range(pairs):
                j = 2 * other + 1 - side
                wait_on(windows[at].at[n, rows_of(j)], kv_got.at[n, at, j])
        turn(n, MAXDOC - 1, MAXDOC - 1 + blocks)

    def turn_halo(n):
        @pl.when(c > 0)
        def _():
            for at in range(2):

                def act(j, low, size, at=at):
                    held = windows[at].at[n, halo_rows(low, size)]
                    wait_on(held, halo_got.at[n, at, j])

                for_pieces(False, act)
            turn(n, 0, MAXDOC - 1)

        @pl.when(c == 0)
        def _():
            for ref in (turned, v_work):
                ref[0 : MAXDOC - 1] = jnp.zeros((MAXDOC - 1,) + ref.shape[1:], ref.dtype)

    causal = lax.broadcasted_iota(jnp.int32, (BLK, BLK), 1) <= lax.broadcasted_iota(
        jnp.int32, (BLK, BLK), 0
    )

    def attend(k, slot):
        block = slot_block[slot]
        count = slot_count[slot]
        queries = q_work[block]
        keys = jnp.concatenate([turned[block + i] for i in range(MAXDOC)], axis=1)
        values = jnp.concatenate([v_work[block + i] for i in range(MAXDOC)], axis=0)
        scores = jnp.dot(queries, keys, preferred_element_type=jnp.float32)
        parts = [scores[:, i * BLK : (i + 1) * BLK] for i in range(MAXDOC)]
        for i in range(MAXDOC - 1):
            inside = jnp.full((BLK, BLK), count - (MAXDOC - 1 - i), jnp.int32) > 0
            parts[i] = jnp.where(inside, parts[i], -jnp.inf)
        parts[-1] = jnp.where(causal, parts[-1], -jnp.inf)
        top = jnp.max(functools.reduce(jnp.maximum, parts), axis=1, keepdims=True)
        parts = [jnp.exp2((x - top) * factor) for x in parts]
        total = jnp.sum(functools.reduce(jnp.add, parts), axis=1, keepdims=True)
        weights = jnp.concatenate([x.astype(jnp.bfloat16) for x in parts], axis=1)
        mixed = jnp.dot(weights, values, preferred_element_type=jnp.float32) / total
        out[k, slot] = mixed.astype(out.dtype)

    def owner(k):
        return 2 * pair + lax.div(lax.div(k, half), kv_heads)

    def column(k):
        n, i = lax.div(k, half), lax.rem(k, half)
        return lax.rem(n, kv_heads) * 2 * half + side * half + i

    def columns(col):
        return pl.ds(aligned(col * HD), HD)

    def target_of(s):
        away = nc // 2 + (1 - 2 * lax.rem(s, 2)) * lax.div(s + 1, 2)
        return lax.rem(c + away, nc)

    def send_out(k, s):
        t = target_of(s)
        col = column(k)
        pltpu.make_async_remote_copy(
            src_ref=out.at[k, pl.ds(t * cap, cap)],
            dst_ref=got_ref.at[pl.ds(c * cap, cap), :, columns(col)],
            send_sem=out_sent.at[k],
            recv_sem=out_got.at[col],
            device_id=(t, owner(k)),
            device_id_type=MESH,
        ).start()

    own_slots = pl.ds(c * cap, cap)

    def send_own(k):
        col = column(k)
        src = out.at[k, own_slots]
        dst = got_ref.at[own_slots, :, columns(col)]

        @pl.when(owner(k) == h)
        def _():
            pltpu.make_async_copy(src, dst, own_got.at[col]).start()

        @pl.when(owner(k) != h)
        def _():
            pltpu.make_async_remote_copy(
                src_ref=src,
                dst_ref=dst,
                send_sem=own_sent.at[k],
                recv_sem=own_got.at[col],
                device_id=(c, partner),
                device_id_type=MESH,
            ).start()

    def head_step(k):
        for j in range(nh):
            wait_on(q_in.at[k, pl.ds(j * part, part)], q_got.at[k, j])
        q_work[...] = q_in[k].reshape(q_work.shape)

        def target(s, carry):
            t = target_of(s)
            for r in range(cap):
                attend(k, t * cap + r)
                if r == 0:

                    @pl.when(s > 0)
                    def _():
                        send_out(k, s - 1)

            return carry

        lax.fori_loop(0, nc, target, 0)
        send_own(k)

    collect(0)
    turn_rows(0)
    pass_halo(0)
    turn_halo(0)

    def one(k, carry):
        n, i = lax.div(k, half), lax.rem(k, half)

        @pl.when((i == 0) & (n > 0))
        def _():
            turn_rows(n)
            turn_halo(n)

        head_step(k)
        def after(head, act):
            pl.when(k == head)(act)

        for later in range(2, shared):
            after(later - 2, functools.partial(lead, later, jnp.logical_not(odd)))
        for later in range(DIRECT, shared):
            after(later - DIRECT, functools.partial(relay, later))
            after(later, functools.partial(spread, later))

        @pl.when(k + AHEAD < heads)
        def _():
            send_q(k + AHEAD)

        for later in range(1, min(DIRECT, shared)):
            after(2 * later - 1, functools.partial(detour_on, later))
        for later in range(1, shared):
            after(2 * later - 2, functools.partial(collect, later))
            last = later * half - 1
            after(last - 1 if later == 1 else last, functools.partial(pass_halo, later))
        return carry

    lax.fori_loop(0, heads, one, 0)

    def settle_kv(n):
        for at in range(2):
            for d in range(pairs):
                wait_on(windows[at].at[n, rows_of(h)], kv_sent.at[n, at, d])
                if d:
                    pass_kv_copy(n, at, d).wait_send()

            @pl.when(c > 0)
            def _(at=at):
                for_pieces(True, lambda *p: pass_halo_copy(n, at, *p).wait_send())

            def sent(j, low, size, at=at):
                wait_on(windows[at].at[n, halo_rows(low, size)], halo_sent.at[n, at, j])

            @pl.when(has_next)
            def _(sent=sent):
                if n >= DIRECT:
                    for_own_pieces(sent)
                else:
                    for_pieces(True, sent)

        if 0 < n < DIRECT:

            @pl.when(relays)
            def _():
                def sent_on(j, low, size):
                    @pl.when(h != j)
                    def _():
                        wait_on(
                            via.at[1, n - 1, halo_rows(low, size)], via_sent.at[1, n - 1, j]
                        )

                for_pieces(True, sent_on)

        if n >= DIRECT:

            def for_places(act):
                for_own_pieces(
                    lambda *p: for_other_pairs(lambda at, d: act(at, place_of(n, d), *p))
                )

            def settled(buffer, sems):
                def act(at, q, j, low, size):
                    wait_on(buffer.at[at, q, halo_rows(low, size)], sems.at[at, q, j])

                return act

            for cond, buffer, sems in (
                (has_next, stage, away_sent),
                (relays, via, via_sent),
                (c > 0, stage, stage_sent),
            ):

                @pl.when(cond)
                def _(buffer=buffer, sems=sems):
                    for_places(settled(buffer, sems))

    for n in range(shared):
        settle_kv(n)

    def drain(k, carry):
        for d in range(1, nh):
            wait_on(q_in.at[k, my_rows], q_sent.at[k, d])

        @pl.when(owner(k) != h)
        def _():
            wait_on(out.at[k, own_slots], own_sent.at[k])

        wait_on(out.at[k, pl.ds(0, (nc - 1) * cap)], out_sent.at[k])
        wait_on(got_ref.at[own_slots, :, columns(k)], own_got.at[k])
        wait_on(got_ref.at[pl.ds(0, (nc - 1) * cap), :, columns(k)], out_got.at[k])
        return carry

    lax.fori_loop(0, heads, drain, 0)


def fused(doc_ids, plan, query, key, value):
    nc, nh = lax.axis_size("ctx"), lax.axis_size("head")
    part = query.shape[0]
    rows = nh * part
    blocks = rows // BLK
    heads = query.shape[1] // nh // HD
    kv_heads = key.shape[1] // nh // HD
    shared = 2 * kv_heads
    places = max(DIRECT - 1, (nh // 2 - 1) * (shared - DIRECT))
    cap = -(-blocks // nc)
    slots = nc * cap
    window = HALO + rows
    dma = pltpu.SemaphoreType.DMA
    buffers = [
        (shared, window, HD),
        (shared, window, HD),
        (2, places, HALO, HD),
        (2, places, HALO, HD),
        (heads, rows, HD),
        (blocks, BLK, HD),
        (window // BLK, HD, BLK),
        (window // BLK, BLK, HD),
        (heads, slots, BLK, HD),
    ]
    held = 2 * sum(math.prod(shape) for shape in buffers)
    return pl.pallas_call(
        functools.partial(fused_kernel, kv_heads, cap),
        out_shape=[
            jax.ShapeDtypeStruct((slots, BLK, heads * HD), query.dtype),
            jax.ShapeDtypeStruct((blocks,), jnp.int32),
        ],
        in_specs=[pl.BlockSpec(memory_space=pltpu.SMEM)] * 2
        + [pl.BlockSpec(memory_space=pltpu.HBM)] * 3,
        out_specs=[
            pl.BlockSpec(memory_space=pl.ANY),
            pl.BlockSpec(memory_space=pltpu.SMEM),
        ],
        scratch_shapes=[pltpu.SMEM((slots,), jnp.int32)] * 2
        + [pltpu.VMEM(shape, query.dtype) for shape in buffers]
        + [dma((heads, nh))] * 2
        + [dma((shared, 2, nh))] * 6
        + [dma((2, places, nh))] * 5
        + [dma((heads,))] * 4
        + [pltpu.SemaphoreType.REGULAR((nc.bit_length(), 2))],
        compiler_params=pltpu.CompilerParams(
            collective_id=0, has_side_effects=True, vmem_limit_bytes=held + (6 << 20)
        ),
        name="fused",
    )(doc_ids, plan, query, key, value)


def place_kernel(mine_ref, got_ref, o_ref, sems):
    copies = []
    for i in range(o_ref.shape[0] // BLK):
        copy = pltpu.make_async_copy(
            got_ref.at[mine_ref[i]], o_ref.at[pl.ds(i * BLK, BLK)], sems.at[i]
        )
        copy.start()
        copies.append(copy)
    for copy in copies:
        copy.wait()


def place(mine, got):
    blocks = mine.shape[0]
    width = got.shape[2]
    return pl.pallas_call(
        place_kernel,
        out_shape=jax.ShapeDtypeStruct((blocks * BLK, width), got.dtype),
        in_specs=[
            pl.BlockSpec(memory_space=pltpu.SMEM),
            pl.BlockSpec(memory_space=pl.ANY),
        ],
        out_specs=pl.BlockSpec(memory_space=pl.ANY),
        scratch_shapes=[pltpu.SemaphoreType.DMA((blocks,))],
        compiler_params=pltpu.CompilerParams(vmem_limit_bytes=1 << 20),
        name="place",
    )(mine, got)


def shards(query, key, value, doc_ids, plan):
    operands = [
        pltpu.with_memory_space_constraint(x, pltpu.HBM)
        for x in (doc_ids, plan, query, key, value)
    ]
    got, mine = fused(*operands)
    return place(mine, got)


def solution(mesh):
    return jax.shard_map(
        shards,
        mesh=mesh,
        in_specs=(
            P(("ctx", "head"), None),
            P(("ctx", "head"), None),
            P(("ctx", "head"), None),
            P(),
            P(),
        ),
        out_specs=P("ctx", "head"),
        check_vma=False,
    )
```

```python
import functools
import math

import jax
import jax.numpy as jnp
from jax import lax
from jax.experimental import pallas as pl
from jax.experimental.pallas import tpu as pltpu
from jax.sharding import PartitionSpec as P

HD = 128
BLK = 128
MAXDOC = 8
HALO = (MAXDOC - 1) * BLK
AHEAD = 8
DIRECT = 3
MESH = pl.DeviceIdType.MESH


def aligned(x):
    return pl.multiple_of(x, BLK)


def fused_kernel(
    kv_heads,
    cap,
    doc_hbm,
    plan_hbm,
    q_ref,
    k_ref,
    v_ref,
    got_ref,
    mine_out,
    doc_ref,
    plan_ref,
    mine_ref,
    slot_block,
    slot_count,
    keys_in,
    values_in,
    via,
    stage,
    q_in,
    q_work,
    turned,
    v_work,
    out,
    q_sent,
    q_got,
    kv_sent,
    kv_passed,
    kv_got,
    halo_sent,
    halo_passed,
    halo_got,
    away_sent,
    via_got,
    via_sent,
    stage_got,
    stage_sent,
    out_sent,
    out_got,
    own_sent,
    own_got,
    index_sems,
    ready,
):
    c, h = lax.axis_index("ctx"), lax.axis_index("head")
    nc, nh = lax.axis_size("ctx"), lax.axis_size("head")
    pairs = nh // 2
    pair, side = lax.div(h, 2), lax.rem(h, 2)
    partner = h + 1 - 2 * side
    part = q_ref.shape[0]
    rows = nh * part
    blocks = rows // BLK
    heads = q_in.shape[0]
    shared = 2 * kv_heads
    half = heads // shared
    factor = math.log2(math.e) / math.sqrt(HD)
    sources = (k_ref, v_ref)
    windows = (keys_in, values_in)

    barrier = pltpu.get_barrier_semaphore()
    for d in range(1, nh):
        pl.semaphore_signal(
            barrier, inc=1, device_id=(c, lax.rem(h + d, nh)), device_id_type=MESH
        )

    @pl.when(c > 0)
    def _():
        pl.semaphore_signal(barrier, inc=1, device_id=(c - 1, h), device_id_type=MESH)

    @pl.when(c < nc - 1)
    def _():
        pl.semaphore_signal(barrier, inc=1, device_id=(c + 1, h), device_id_type=MESH)

    index_copies = [
        pltpu.make_async_copy(doc_hbm, doc_ref, index_sems.at[0]),
        pltpu.make_async_copy(plan_hbm, plan_ref, index_sems.at[1]),
    ]
    mine_copy = pltpu.make_async_copy(mine_ref, mine_out, index_sems.at[2])
    for copy in index_copies:
        copy.start()
    near = jnp.where(c > 0, 1, 0) + jnp.where(c < nc - 1, 1, 0)
    pl.semaphore_wait(barrier, nh - 1 + near)

    my_rows = pl.ds(aligned(h * part), part)

    def rows_of(j):
        return pl.ds(aligned(HALO + j * part), part)

    def wait_on(ref, sem):
        pltpu.make_async_copy(ref, ref, sem).wait()

    def send_kv(n):
        for at in range(2):
            dst = windows[at].at[n, rows_of(h)]
            for d in range(pairs):
                other = lax.rem(pair + d, pairs)
                pltpu.make_async_remote_copy(
                    src_ref=sources[at].at[:, pl.ds(aligned((other * shared + n) * HD), HD)],
                    dst_ref=dst,
                    send_sem=kv_sent.at[n, at, d],
                    recv_sem=kv_got.at[n, at, h],
                    device_id=(c, 2 * other + side if d else partner),
                    device_id_type=MESH,
                ).start()
            pltpu.make_async_copy(
                sources[at].at[:, pl.ds(aligned((pair * shared + n) * HD), HD)],
                dst,
                kv_got.at[n, at, h],
            ).start()

    def q_columns(k, t):
        pair_of, side_of = lax.div(t, 2), lax.rem(t, 2)
        n, i = lax.div(k, half), lax.rem(k, half)
        first = 2 * pair_of * heads + n * 2 * half + side_of * half + i
        return pl.ds(aligned(first * HD), HD)

    def send_q(k):
        for d in range(1, nh):
            t = lax.rem(h + d, nh)
            pltpu.make_async_remote_copy(
                src_ref=q_ref.at[:, q_columns(k, t)],
                dst_ref=q_in.at[k, my_rows],
                send_sem=q_sent.at[k, d],
                recv_sem=q_got.at[k, h],
                device_id=(c, t),
                device_id_type=MESH,
            ).start()
        pltpu.make_async_copy(
            q_ref.at[:, q_columns(k, h)], q_in.at[k, my_rows], q_got.at[k, h]
        ).start()

    pieces = []
    for j in range(nh - 1, -1, -1):
        low, high = max(rows - HALO, j * part), (j + 1) * part
        if low < high:
            pieces.append((j, low, high - low))

    odd = lax.rem(c, 2) == 1
    has_next = c < nc - 1
    following = jnp.minimum(c + 1, nc - 1)
    relays = jnp.logical_not(odd) & (c + 2 < nc)

    def for_pieces(mine, act):
        for j, low, size in pieces:

            @pl.when((side == j % 2) if mine else (side != j % 2))
            def _(j=j, low=low, size=size):
                act(j, low, size)

    def for_own_pieces(act):
        for j, low, size in pieces:

            @pl.when(h == j)
            def _(j=j, low=low, size=size):
                act(j, low, size)

    def for_other_pairs(act):
        for at in range(2):
            for d in range(1, pairs):
                act(at, d)

    def halo_rows(low, size):
        return pl.ds(HALO + low - rows, size)

    def rows_in(at, n, d, j, low, size):
        other = lax.rem(pair + d, pairs)
        return sources[at].at[
            pl.ds(low - j * part, size), pl.ds(aligned((other * shared + n) * HD), HD)
        ]

    def halo_copy(n, at, j, low, size, src):
        return pltpu.make_async_remote_copy(
            src_ref=src,
            dst_ref=windows[at].at[n, halo_rows(low, size)],
            send_sem=halo_sent.at[n, at, j],
            recv_sem=halo_got.at[n, at, j],
            device_id=(following, h),
            device_id_type=MESH,
        )

    def place_of(n, d):
        return (d - 1) * (shared - DIRECT) + n - DIRECT

    def away_copy(n, at, d, j, low, size, back):
        q = place_of(n, d)
        return pltpu.make_async_remote_copy(
            src_ref=rows_in(at, n, d, j, low, size),
            dst_ref=(via if back else stage).at[at, q, halo_rows(low, size)],
            send_sem=away_sent.at[at, q, j],
            recv_sem=(via_got if back else stage_got).at[at, q, j],
            device_id=(jnp.maximum(c - 1, 0) if back else following, h),
            device_id_type=MESH,
        )

    def lead(n, who):
        @pl.when(has_next & who)
        def _():
            def own_pair(j, low, size):
                for at in range(2):
                    src = rows_in(at, n, 0, j, low, size)
                    halo_copy(n, at, j, low, size, src).start()

            for_own_pieces(own_pair)

        if n >= DIRECT:
            for back, turn_of in ((True, odd), (False, jnp.logical_not(odd))):

                @pl.when(has_next & who & turn_of)
                def _(back=back):
                    for_own_pieces(
                        lambda *p: for_other_pairs(
                            lambda at, d: away_copy(n, at, d, *p, back).start()
                        )
                    )

    def send_kv_after(k):
        for n in range(1, shared):
            if k == 2 * n - 2:
                send_kv(n)

    always = c >= 0
    lead(0, always)
    send_kv(0)
    for k in range(min(AHEAD, heads)):
        send_q(k)
        send_kv_after(k)
        if k == 0:
            for n in range(1, shared):
                lead(n, always if n == 1 else odd)

    step, d = 0, 1
    while d < nc:
        below, above = c >= d, c + d < nc
        for there, other, mark in ((below, c - d, 1), (above, c + d, 0)):

            @pl.when(there)
            def _(other=other, mark=mark, step=step):
                pl.semaphore_signal(
                    ready.at[step, mark], inc=1, device_id=(other, h), device_id_type=MESH
                )

        for there, mark in ((below, 0), (above, 1)):

            @pl.when(there)
            def _(mark=mark, step=step):
                pl.semaphore_wait(ready.at[step, mark], 1)

        step, d = step + 1, 2 * d

    for copy in index_copies:
        copy.wait()

    def table(k, carry):
        found = [jnp.int32(0)] * cap
        seen = jnp.int32(0)
        for i in range(blocks):
            p = plan_ref[k * blocks + i]
            hit = lax.div(p, blocks) == c
            for r in range(cap):
                found[r] = jnp.where(hit & (seen == r), lax.rem(p, blocks), found[r])
            seen = seen + jnp.where(hit, 1, 0)
        for r in range(cap):
            at = c * blocks + found[r]
            document = doc_ref[at]
            count = jnp.int32(1)
            for t in range(1, MAXDOC):
                same = doc_ref[jnp.maximum(at - t, 0)] == document
                count = count + jnp.where((at >= t) & same, 1, 0)
            slot_block[k * cap + r] = found[r]
            slot_count[k * cap + r] = count
        return carry

    lax.fori_loop(0, nc, table, 0)

    origins = [lax.div(plan_ref[c * blocks + i], blocks) for i in range(blocks)]
    for i in range(blocks):
        rank = jnp.int32(0)
        for before in range(i):
            rank = rank + jnp.where(origins[before] == origins[i], 1, 0)
        mine_ref[i] = origins[i] * cap + jnp.minimum(rank, cap - 1)
    mine_copy.start()

    def pass_halo_copy(n, at, j, low, size):
        ref = windows[at].at[n, halo_rows(low, size)]
        return pltpu.make_async_remote_copy(
            src_ref=ref,
            dst_ref=ref,
            send_sem=halo_passed.at[n, at, j],
            recv_sem=halo_got.at[n, at, j],
            device_id=(c, partner),
            device_id_type=MESH,
        )

    def pass_kv_copy(n, at, d):
        j = 2 * lax.rem(pair + d, pairs) + side
        ref = windows[at].at[n, rows_of(j)]
        return pltpu.make_async_remote_copy(
            src_ref=ref,
            dst_ref=ref,
            send_sem=kv_passed.at[n, at, d],
            recv_sem=kv_got.at[n, at, j],
            device_id=(c, partner),
            device_id_type=MESH,
        )

    def collect(n):
        for at in range(2):
            for d in range(pairs):
                j = 2 * lax.rem(pair + d, pairs) + side
                wait_on(windows[at].at[n, rows_of(j)], kv_got.at[n, at, j])
                if d:
                    pass_kv_copy(n, at, d).start()
            if n >= DIRECT:
                continue

            def act(j, low, size, at=at):
                @pl.when((h != j) & (odd if n and at else False))
                def _():
                    detour_copy(n, j, low, size).start()

                @pl.when((h != j) & jnp.logical_not(odd if n and at else False))
                def _():
                    src = windows[at].at[n, pl.ds(HALO + low, size)]
                    halo_copy(n, at, j, low, size, src).start()

            @pl.when(has_next)
            def _(act=act):
                for_pieces(True, act)

    def detour_copy(n, j, low, size):
        return pltpu.make_async_remote_copy(
            src_ref=values_in.at[n, pl.ds(HALO + low, size)],
            dst_ref=via.at[1, n - 1, halo_rows(low, size)],
            send_sem=halo_sent.at[n, 1, j],
            recv_sem=via_got.at[1, n - 1, j],
            device_id=(jnp.maximum(c - 1, 0), h),
            device_id_type=MESH,
        )

    def detour_on_copy(n, j, low, size):
        held = halo_rows(low, size)
        return pltpu.make_async_remote_copy(
            src_ref=via.at[1, n - 1, held],
            dst_ref=values_in.at[n, held],
            send_sem=via_sent.at[1, n - 1, j],
            recv_sem=halo_got.at[n, 1, j],
            device_id=(jnp.minimum(c + 2, nc - 1), h),
            device_id_type=MESH,
        )

    def detour_on(n):
        @pl.when(relays)
        def _():
            def act(j, low, size):
                @pl.when(h != j)
                def _():
                    wait_on(via.at[1, n - 1, halo_rows(low, size)], via_got.at[1, n - 1, j])
                    detour_on_copy(n, j, low, size).start()

            for_pieces(True, act)

    def relay_copy(n, at, d, j, low, size):
        q = place_of(n, d)
        held = halo_rows(low, size)
        return pltpu.make_async_remote_copy(
            src_ref=via.at[at, q, held],
            dst_ref=stage.at[at, q, held],
            send_sem=via_sent.at[at, q, j],
            recv_sem=stage_got.at[at, q, j],
            device_id=(jnp.minimum(c + 2, nc - 1), h),
            device_id_type=MESH,
        )

    def relay(n):
        @pl.when(relays)
        def _():
            def act(j, low, size):
                def one_of(at, d):
                    q = place_of(n, d)
                    wait_on(via.at[at, q, halo_rows(low, size)], via_got.at[at, q, j])
                    relay_copy(n, at, d, j, low, size).start()

                for_other_pairs(one_of)

            for_own_pieces(act)

    def spread_copy(n, at, d, j, low, size):
        q = place_of(n, d)
        held = halo_rows(low, size)
        return pltpu.make_async_remote_copy(
            src_ref=stage.at[at, q, held],
            dst_ref=windows[at].at[n, held],
            send_sem=stage_sent.at[at, q, j],
            recv_sem=halo_got.at[n, at, j],
            device_id=(c, 2 * lax.rem(pair + d, pairs) + side),
            device_id_type=MESH,
        )

    def spread(n):
        @pl.when(c > 0)
        def _():
            def act(j, low, size):
                def one_of(at, d):
                    q = place_of(n, d)
                    wait_on(stage.at[at, q, halo_rows(low, size)], stage_got.at[at, q, j])
                    spread_copy(n, at, d, j, low, size).start()

                for_other_pairs(one_of)

            for_own_pieces(act)

    def pass_halo(n):
        @pl.when(c > 0)
        def _():
            for at in range(2):

                def act(j, low, size, at=at):
                    held = windows[at].at[n, halo_rows(low, size)]
                    wait_on(held, halo_got.at[n, at, j])
                    pass_halo_copy(n, at, j, low, size).start()

                for_pieces(True, act)

    def turn(n, first, last):
        for i in range(first, last):
            turned[i] = keys_in[n, i * BLK : (i + 1) * BLK, :].T
            v_work[i] = values_in[n, i * BLK : (i + 1) * BLK, :]

    def turn_rows(n):
        for at in range(2):
            for other in range(pairs):
                j = 2 * other + 1 - side
                wait_on(windows[at].at[n, rows_of(j)], kv_got.at[n, at, j])
        turn(n, MAXDOC - 1, MAXDOC - 1 + blocks)

    def turn_halo(n):
        @pl.when(c > 0)
        def _():
            for at in range(2):

                def act(j, low, size, at=at):
                    held = windows[at].at[n, halo_rows(low, size)]
                    wait_on(held, halo_got.at[n, at, j])

                for_pieces(False, act)
            turn(n, 0, MAXDOC - 1)

        @pl.when(c == 0)
        def _():
            for ref in (turned, v_work):
                ref[0 : MAXDOC - 1] = jnp.zeros((MAXDOC - 1,) + ref.shape[1:], ref.dtype)

    causal = lax.broadcasted_iota(jnp.int32, (BLK, BLK), 1) <= lax.broadcasted_iota(
        jnp.int32, (BLK, BLK), 0
    )

    def attend(k, slot):
        block = slot_block[slot]
        count = slot_count[slot]
        queries = q_work[block]
        keys = jnp.concatenate([turned[block + i] for i in range(MAXDOC)], axis=1)
        values = jnp.concatenate([v_work[block + i] for i in range(MAXDOC)], axis=0)
        scores = jnp.dot(queries, keys, preferred_element_type=jnp.float32)
        parts = [scores[:, i * BLK : (i + 1) * BLK] for i in range(MAXDOC)]
        for i in range(MAXDOC - 1):
            inside = jnp.full((BLK, BLK), count - (MAXDOC - 1 - i), jnp.int32) > 0
            parts[i] = jnp.where(inside, parts[i], -jnp.inf)
        parts[-1] = jnp.where(causal, parts[-1], -jnp.inf)
        top = jnp.max(functools.reduce(jnp.maximum, parts), axis=1, keepdims=True)
        parts = [jnp.exp2((x - top) * factor) for x in parts]
        total = jnp.sum(functools.reduce(jnp.add, parts), axis=1, keepdims=True)
        weights = jnp.concatenate([x.astype(jnp.bfloat16) for x in parts], axis=1)
        mixed = jnp.dot(weights, values, preferred_element_type=jnp.float32) / total
        out[k, slot] = mixed.astype(out.dtype)

    def owner(k):
        return 2 * pair + lax.div(lax.div(k, half), kv_heads)

    def column(k):
        n, i = lax.div(k, half), lax.rem(k, half)
        return lax.rem(n, kv_heads) * 2 * half + side * half + i

    def columns(col):
        return pl.ds(aligned(col * HD), HD)

    def target_of(s):
        away = nc // 2 + (1 - 2 * lax.rem(s, 2)) * lax.div(s + 1, 2)
        return lax.rem(c + away, nc)

    def send_out(k, s):
        t = target_of(s)
        col = column(k)
        pltpu.make_async_remote_copy(
            src_ref=out.at[k, pl.ds(t * cap, cap)],
            dst_ref=got_ref.at[pl.ds(c * cap, cap), :, columns(col)],
            send_sem=out_sent.at[k],
            recv_sem=out_got.at[col],
            device_id=(t, owner(k)),
            device_id_type=MESH,
        ).start()

    own_slots = pl.ds(c * cap, cap)

    def send_own(k):
        col = column(k)
        src = out.at[k, own_slots]
        dst = got_ref.at[own_slots, :, columns(col)]

        @pl.when(owner(k) == h)
        def _():
            pltpu.make_async_copy(src, dst, own_got.at[col]).start()

        @pl.when(owner(k) != h)
        def _():
            pltpu.make_async_remote_copy(
                src_ref=src,
                dst_ref=dst,
                send_sem=own_sent.at[k],
                recv_sem=own_got.at[col],
                device_id=(c, partner),
                device_id_type=MESH,
            ).start()

    def head_step(k):
        for j in range(nh):
            wait_on(q_in.at[k, pl.ds(j * part, part)], q_got.at[k, j])
        q_work[...] = q_in[k].reshape(q_work.shape)

        def target(s, carry):
            t = target_of(s)
            for r in range(cap):
                attend(k, t * cap + r)
                if r == 0:

                    @pl.when(s > 0)
                    def _():
                        send_out(k, s - 1)

            return carry

        lax.fori_loop(0, nc, target, 0)
        send_own(k)

    collect(0)
    turn_rows(0)
    pass_halo(0)
    turn_halo(0)

    def one(k, carry):
        n, i = lax.div(k, half), lax.rem(k, half)

        @pl.when((i == 0) & (n > 0))
        def _():
            turn_rows(n)
            turn_halo(n)

        head_step(k)
        def after(head, act):
            pl.when(k == head)(act)

        for later in range(2, shared):
            after(later - 2, functools.partial(lead, later, jnp.logical_not(odd)))
        for later in range(DIRECT, shared):
            after(later - DIRECT, functools.partial(relay, later))
            after(later, functools.partial(spread, later))

        @pl.when(k + AHEAD < heads)
        def _():
            send_q(k + AHEAD)

        for later in range(1, min(DIRECT, shared)):
            after(2 * later - 1, functools.partial(detour_on, later))
        for later in range(1, shared):
            after(2 * later - 2, functools.partial(collect, later))
            last = later * half - 1
            after(last - 1 if later == 1 else last, functools.partial(pass_halo, later))
        return carry

    lax.fori_loop(0, heads, one, 0)

    def settle_kv(n):
        for at in range(2):
            for d in range(pairs):
                wait_on(windows[at].at[n, rows_of(h)], kv_sent.at[n, at, d])
                if d:
                    pass_kv_copy(n, at, d).wait_send()

            @pl.when(c > 0)
            def _(at=at):
                for_pieces(True, lambda *p: pass_halo_copy(n, at, *p).wait_send())

            def sent(j, low, size, at=at):
                wait_on(windows[at].at[n, halo_rows(low, size)], halo_sent.at[n, at, j])

            @pl.when(has_next)
            def _(sent=sent):
                if n >= DIRECT:
                    for_own_pieces(sent)
                else:
                    for_pieces(True, sent)

        if 0 < n < DIRECT:

            @pl.when(relays)
            def _():
                def sent_on(j, low, size):
                    @pl.when(h != j)
                    def _():
                        wait_on(
                            via.at[1, n - 1, halo_rows(low, size)], via_sent.at[1, n - 1, j]
                        )

                for_pieces(True, sent_on)

        if n >= DIRECT:

            def for_places(act):
                for_own_pieces(
                    lambda *p: for_other_pairs(lambda at, d: act(at, place_of(n, d), *p))
                )

            def settled(buffer, sems):
                def act(at, q, j, low, size):
                    wait_on(buffer.at[at, q, halo_rows(low, size)], sems.at[at, q, j])

                return act

            for cond, buffer, sems in (
                (has_next, stage, away_sent),
                (relays, via, via_sent),
                (c > 0, stage, stage_sent),
            ):

                @pl.when(cond)
                def _(buffer=buffer, sems=sems):
                    for_places(settled(buffer, sems))

    for n in range(shared):
        settle_kv(n)

    mine_copy.wait()

    def drain(k, carry):
        for d in range(1, nh):
            wait_on(q_in.at[k, my_rows], q_sent.at[k, d])

        @pl.when(owner(k) != h)
        def _():
            wait_on(out.at[k, own_slots], own_sent.at[k])

        wait_on(out.at[k, pl.ds(0, (nc - 1) * cap)], out_sent.at[k])
        wait_on(got_ref.at[own_slots, :, columns(k)], own_got.at[k])
        wait_on(got_ref.at[pl.ds(0, (nc - 1) * cap), :, columns(k)], out_got.at[k])
        return carry

    lax.fori_loop(0, heads, drain, 0)


def fused(doc_ids, plan, query, key, value):
    nc, nh = lax.axis_size("ctx"), lax.axis_size("head")
    part = query.shape[0]
    rows = nh * part
    blocks = rows // BLK
    heads = query.shape[1] // nh // HD
    kv_heads = key.shape[1] // nh // HD
    shared = 2 * kv_heads
    places = max(DIRECT - 1, (nh // 2 - 1) * (shared - DIRECT))
    cap = -(-blocks // nc)
    slots = nc * cap
    window = HALO + rows
    dma = pltpu.SemaphoreType.DMA
    buffers = [
        (shared, window, HD),
        (shared, window, HD),
        (2, places, HALO, HD),
        (2, places, HALO, HD),
        (heads, rows, HD),
        (blocks, BLK, HD),
        (window // BLK, HD, BLK),
        (window // BLK, BLK, HD),
        (heads, slots, BLK, HD),
    ]
    held = 2 * sum(math.prod(shape) for shape in buffers)
    return pl.pallas_call(
        functools.partial(fused_kernel, kv_heads, cap),
        out_shape=[
            jax.ShapeDtypeStruct((slots, BLK, heads * HD), query.dtype),
            jax.ShapeDtypeStruct((blocks,), jnp.int32),
        ],
        in_specs=[pl.BlockSpec(memory_space=pltpu.HBM)] * 5,
        out_specs=[pl.BlockSpec(memory_space=pl.ANY)] * 2,
        scratch_shapes=[
            pltpu.SMEM(n, jnp.int32)
            for n in (doc_ids.shape, plan.shape, (blocks,), (slots,), (slots,))
        ]
        + [pltpu.VMEM(shape, query.dtype) for shape in buffers]
        + [dma((heads, nh))] * 2
        + [dma((shared, 2, nh))] * 6
        + [dma((2, places, nh))] * 5
        + [dma((heads,))] * 4
        + [dma((3,))]
        + [pltpu.SemaphoreType.REGULAR((nc.bit_length(), 2))],
        compiler_params=pltpu.CompilerParams(
            collective_id=0, has_side_effects=True, vmem_limit_bytes=held + (6 << 20)
        ),
        name="fused",
    )(doc_ids, plan, query, key, value)


def place_kernel(mine_ref, got_ref, o_ref, sems):
    copies = []
    for i in range(o_ref.shape[0] // BLK):
        copy = pltpu.make_async_copy(
            got_ref.at[mine_ref[i]], o_ref.at[pl.ds(i * BLK, BLK)], sems.at[i]
        )
        copy.start()
        copies.append(copy)
    for copy in copies:
        copy.wait()


def place(mine, got):
    blocks = mine.shape[0]
    width = got.shape[2]
    return pl.pallas_call(
        place_kernel,
        out_shape=jax.ShapeDtypeStruct((blocks * BLK, width), got.dtype),
        in_specs=[
            pl.BlockSpec(memory_space=pltpu.SMEM),
            pl.BlockSpec(memory_space=pl.ANY),
        ],
        out_specs=pl.BlockSpec(memory_space=pl.ANY),
        scratch_shapes=[pltpu.SemaphoreType.DMA((blocks,))],
        compiler_params=pltpu.CompilerParams(vmem_limit_bytes=1 << 20),
        name="place",
    )(mine, got)


def shards(query, key, value, doc_ids, plan):
    operands = [
        pltpu.with_memory_space_constraint(x, pltpu.HBM)
        for x in (doc_ids, plan, query, key, value)
    ]
    got, mine = fused(*operands)
    return place(mine, got)


def solution(mesh):
    return jax.shard_map(
        shards,
        mesh=mesh,
        in_specs=(
            P(("ctx", "head"), None),
            P(("ctx", "head"), None),
            P(("ctx", "head"), None),
            P(),
            P(),
        ),
        out_specs=P("ctx", "head"),
        check_vma=False,
    )
```

```python
import functools
import math

import jax
import jax.numpy as jnp
from jax import lax
from jax.experimental import pallas as pl
from jax.experimental.pallas import tpu as pltpu
from jax.sharding import PartitionSpec as P

HD = 128
BLK = 128
MAXDOC = 8
HALO = (MAXDOC - 1) * BLK
AHEAD = 8
DIRECT = 3
MESH = pl.DeviceIdType.MESH


def aligned(x):
    return pl.multiple_of(x, BLK)


def fused_kernel(
    kv_heads,
    cap,
    doc_hbm,
    plan_hbm,
    q_ref,
    k_ref,
    v_ref,
    got_ref,
    mine_out,
    doc_ref,
    plan_ref,
    mine_ref,
    slot_block,
    slot_count,
    keys_in,
    values_in,
    via,
    stage,
    q_in,
    q_work,
    turned,
    v_work,
    out,
    q_sent,
    q_got,
    kv_sent,
    kv_passed,
    kv_got,
    halo_sent,
    halo_passed,
    halo_got,
    away_sent,
    via_got,
    via_sent,
    stage_got,
    stage_sent,
    out_sent,
    out_got,
    own_sent,
    own_got,
    index_sems,
    ready,
):
    c, h = lax.axis_index("ctx"), lax.axis_index("head")
    nc, nh = lax.axis_size("ctx"), lax.axis_size("head")
    pairs = nh // 2
    pair, side = lax.div(h, 2), lax.rem(h, 2)
    partner = h + 1 - 2 * side
    part = q_ref.shape[0]
    rows = nh * part
    blocks = rows // BLK
    heads = q_in.shape[0]
    shared = 2 * kv_heads
    half = heads // shared
    factor = math.log2(math.e) / math.sqrt(HD)
    sources = (k_ref, v_ref)
    windows = (keys_in, values_in)

    barrier = pltpu.get_barrier_semaphore()
    for d in range(1, nh):
        pl.semaphore_signal(
            barrier, inc=1, device_id=(c, lax.rem(h + d, nh)), device_id_type=MESH
        )

    @pl.when(c > 0)
    def _():
        pl.semaphore_signal(barrier, inc=1, device_id=(c - 1, h), device_id_type=MESH)

    @pl.when(c < nc - 1)
    def _():
        pl.semaphore_signal(barrier, inc=1, device_id=(c + 1, h), device_id_type=MESH)

    index_copies = [
        pltpu.make_async_copy(doc_hbm, doc_ref, index_sems.at[0]),
        pltpu.make_async_copy(plan_hbm, plan_ref, index_sems.at[1]),
    ]
    mine_copy = pltpu.make_async_copy(mine_ref, mine_out, index_sems.at[2])
    for copy in index_copies:
        copy.start()
    near = jnp.where(c > 0, 1, 0) + jnp.where(c < nc - 1, 1, 0)
    pl.semaphore_wait(barrier, nh - 1 + near)

    my_rows = pl.ds(aligned(h * part), part)

    def rows_of(j):
        return pl.ds(aligned(HALO + j * part), part)

    def wait_on(ref, sem):
        pltpu.make_async_copy(ref, ref, sem).wait()

    def send_kv(n):
        for at in range(2):
            dst = windows[at].at[n, rows_of(h)]
            for d in range(pairs):
                other = lax.rem(pair + d, pairs)
                pltpu.make_async_remote_copy(
                    src_ref=sources[at].at[:, pl.ds(aligned((other * shared + n) * HD), HD)],
                    dst_ref=dst,
                    send_sem=kv_sent.at[n, at, d],
                    recv_sem=kv_got.at[n, at, h],
                    device_id=(c, 2 * other + side if d else partner),
                    device_id_type=MESH,
                ).start()
            pltpu.make_async_copy(
                sources[at].at[:, pl.ds(aligned((pair * shared + n) * HD), HD)],
                dst,
                kv_got.at[n, at, h],
            ).start()

    def q_columns(k, t):
        pair_of, side_of = lax.div(t, 2), lax.rem(t, 2)
        n, i = lax.div(k, half), lax.rem(k, half)
        first = 2 * pair_of * heads + n * 2 * half + side_of * half + i
        return pl.ds(aligned(first * HD), HD)

    def send_q(k):
        for d in range(1, nh):
            t = lax.rem(h + d, nh)
            pltpu.make_async_remote_copy(
                src_ref=q_ref.at[:, q_columns(k, t)],
                dst_ref=q_in.at[k, my_rows],
                send_sem=q_sent.at[k, d],
                recv_sem=q_got.at[k, h],
                device_id=(c, t),
                device_id_type=MESH,
            ).start()
        pltpu.make_async_copy(
            q_ref.at[:, q_columns(k, h)], q_in.at[k, my_rows], q_got.at[k, h]
        ).start()

    pieces = []
    for j in range(nh - 1, -1, -1):
        low, high = max(rows - HALO, j * part), (j + 1) * part
        if low < high:
            pieces.append((j, low, high - low))

    odd = lax.rem(c, 2) == 1
    has_next = c < nc - 1
    following = jnp.minimum(c + 1, nc - 1)
    relays = jnp.logical_not(odd) & (c + 2 < nc)

    def for_pieces(mine, act):
        for j, low, size in pieces:

            @pl.when((side == j % 2) if mine else (side != j % 2))
            def _(j=j, low=low, size=size):
                act(j, low, size)

    def for_own_pieces(act):
        for j, low, size in pieces:

            @pl.when(h == j)
            def _(j=j, low=low, size=size):
                act(j, low, size)

    def for_other_pairs(act):
        for at in range(2):
            for d in range(1, pairs):
                act(at, d)

    def halo_rows(low, size):
        return pl.ds(HALO + low - rows, size)

    def rows_in(at, n, d, j, low, size):
        other = lax.rem(pair + d, pairs)
        return sources[at].at[
            pl.ds(low - j * part, size), pl.ds(aligned((other * shared + n) * HD), HD)
        ]

    def halo_copy(n, at, j, low, size, src):
        return pltpu.make_async_remote_copy(
            src_ref=src,
            dst_ref=windows[at].at[n, halo_rows(low, size)],
            send_sem=halo_sent.at[n, at, j],
            recv_sem=halo_got.at[n, at, j],
            device_id=(following, h),
            device_id_type=MESH,
        )

    def place_of(n, d):
        return (d - 1) * (shared - DIRECT) + n - DIRECT

    def away_copy(n, at, d, j, low, size, back):
        q = place_of(n, d)
        return pltpu.make_async_remote_copy(
            src_ref=rows_in(at, n, d, j, low, size),
            dst_ref=(via if back else stage).at[at, q, halo_rows(low, size)],
            send_sem=away_sent.at[at, q, j],
            recv_sem=(via_got if back else stage_got).at[at, q, j],
            device_id=(jnp.maximum(c - 1, 0) if back else following, h),
            device_id_type=MESH,
        )

    def lead(n, who):
        @pl.when(has_next & who)
        def _():
            def own_pair(j, low, size):
                for at in range(2):
                    src = rows_in(at, n, 0, j, low, size)
                    halo_copy(n, at, j, low, size, src).start()

            for_own_pieces(own_pair)

        if n >= DIRECT:
            for back, turn_of in ((True, odd), (False, jnp.logical_not(odd))):

                @pl.when(has_next & who & turn_of)
                def _(back=back):
                    for_own_pieces(
                        lambda *p: for_other_pairs(
                            lambda at, d: away_copy(n, at, d, *p, back).start()
                        )
                    )

    def send_kv_after(k):
        for n in range(1, shared):
            if k == 2 * n - 2:
                send_kv(n)

    always = c >= 0
    lead(0, always)
    send_kv(0)
    for k in range(min(AHEAD, heads)):
        send_q(k)
        send_kv_after(k)
        if k == 0:
            for n in range(1, shared):
                lead(n, always if n == 1 else odd)

    step, d = 0, 1
    while d < nc:
        below, above = c >= d, c + d < nc
        for there, other, mark in ((below, c - d, 1), (above, c + d, 0)):

            @pl.when(there)
            def _(other=other, mark=mark, step=step):
                pl.semaphore_signal(
                    ready.at[step, mark], inc=1, device_id=(other, h), device_id_type=MESH
                )

        for there, mark in ((below, 0), (above, 1)):

            @pl.when(there)
            def _(mark=mark, step=step):
                pl.semaphore_wait(ready.at[step, mark], 1)

        step, d = step + 1, 2 * d

    for copy in index_copies:
        copy.wait()

    def table(k, carry):
        found = [jnp.int32(0)] * cap
        seen = jnp.int32(0)
        for i in range(blocks):
            p = plan_ref[k * blocks + i]
            hit = lax.div(p, blocks) == c
            for r in range(cap):
                found[r] = jnp.where(hit & (seen == r), lax.rem(p, blocks), found[r])
            seen = seen + jnp.where(hit, 1, 0)
        for r in range(cap):
            at = c * blocks + found[r]
            document = doc_ref[at]
            count = jnp.int32(1)
            for t in range(1, MAXDOC):
                same = doc_ref[jnp.maximum(at - t, 0)] == document
                count = count + jnp.where((at >= t) & same, 1, 0)
            slot_block[k * cap + r] = found[r]
            slot_count[k * cap + r] = count
        return carry

    lax.fori_loop(0, nc, table, 0)

    origins = [lax.div(plan_ref[c * blocks + i], blocks) for i in range(blocks)]
    for i in range(blocks):
        rank = jnp.int32(0)
        for before in range(i):
            rank = rank + jnp.where(origins[before] == origins[i], 1, 0)
        mine_ref[i] = origins[i] * cap + jnp.minimum(rank, cap - 1)
    mine_copy.start()

    def pass_halo_copy(n, at, j, low, size):
        ref = windows[at].at[n, halo_rows(low, size)]
        return pltpu.make_async_remote_copy(
            src_ref=ref,
            dst_ref=ref,
            send_sem=halo_passed.at[n, at, j],
            recv_sem=halo_got.at[n, at, j],
            device_id=(c, partner),
            device_id_type=MESH,
        )

    def pass_kv_copy(n, at, d):
        j = 2 * lax.rem(pair + d, pairs) + side
        ref = windows[at].at[n, rows_of(j)]
        return pltpu.make_async_remote_copy(
            src_ref=ref,
            dst_ref=ref,
            send_sem=kv_passed.at[n, at, d],
            recv_sem=kv_got.at[n, at, j],
            device_id=(c, partner),
            device_id_type=MESH,
        )

    def collect(n):
        for at in range(2):
            for d in range(pairs):
                j = 2 * lax.rem(pair + d, pairs) + side
                wait_on(windows[at].at[n, rows_of(j)], kv_got.at[n, at, j])
                if d:
                    pass_kv_copy(n, at, d).start()
            if n >= DIRECT:
                continue

            def act(j, low, size, at=at):
                @pl.when((h != j) & (odd if n and at else False))
                def _():
                    detour_copy(n, j, low, size).start()

                @pl.when((h != j) & jnp.logical_not(odd if n and at else False))
                def _():
                    src = windows[at].at[n, pl.ds(HALO + low, size)]
                    halo_copy(n, at, j, low, size, src).start()

            @pl.when(has_next)
            def _(act=act):
                for_pieces(True, act)

    def detour_copy(n, j, low, size):
        return pltpu.make_async_remote_copy(
            src_ref=values_in.at[n, pl.ds(HALO + low, size)],
            dst_ref=via.at[1, n - 1, halo_rows(low, size)],
            send_sem=halo_sent.at[n, 1, j],
            recv_sem=via_got.at[1, n - 1, j],
            device_id=(jnp.maximum(c - 1, 0), h),
            device_id_type=MESH,
        )

    def detour_on_copy(n, j, low, size):
        held = halo_rows(low, size)
        return pltpu.make_async_remote_copy(
            src_ref=via.at[1, n - 1, held],
            dst_ref=values_in.at[n, held],
            send_sem=via_sent.at[1, n - 1, j],
            recv_sem=halo_got.at[n, 1, j],
            device_id=(jnp.minimum(c + 2, nc - 1), h),
            device_id_type=MESH,
        )

    def detour_on(n):
        @pl.when(relays)
        def _():
            def act(j, low, size):
                @pl.when(h != j)
                def _():
                    wait_on(via.at[1, n - 1, halo_rows(low, size)], via_got.at[1, n - 1, j])
                    detour_on_copy(n, j, low, size).start()

            for_pieces(True, act)

    def relay_copy(n, at, d, j, low, size):
        q = place_of(n, d)
        held = halo_rows(low, size)
        return pltpu.make_async_remote_copy(
            src_ref=via.at[at, q, held],
            dst_ref=stage.at[at, q, held],
            send_sem=via_sent.at[at, q, j],
            recv_sem=stage_got.at[at, q, j],
            device_id=(jnp.minimum(c + 2, nc - 1), h),
            device_id_type=MESH,
        )

    def relay(n):
        @pl.when(relays)
        def _():
            def act(j, low, size):
                def one_of(at, d):
                    q = place_of(n, d)
                    wait_on(via.at[at, q, halo_rows(low, size)], via_got.at[at, q, j])
                    relay_copy(n, at, d, j, low, size).start()

                for_other_pairs(one_of)

            for_own_pieces(act)

    def spread_copy(n, at, d, j, low, size):
        q = place_of(n, d)
        held = halo_rows(low, size)
        return pltpu.make_async_remote_copy(
            src_ref=stage.at[at, q, held],
            dst_ref=windows[at].at[n, held],
            send_sem=stage_sent.at[at, q, j],
            recv_sem=halo_got.at[n, at, j],
            device_id=(c, 2 * lax.rem(pair + d, pairs) + side),
            device_id_type=MESH,
        )

    def spread(n):
        @pl.when(c > 0)
        def _():
            def act(j, low, size):
                def one_of(at, d):
                    q = place_of(n, d)
                    wait_on(stage.at[at, q, halo_rows(low, size)], stage_got.at[at, q, j])
                    spread_copy(n, at, d, j, low, size).start()

                for_other_pairs(one_of)

            for_own_pieces(act)

    def pass_halo(n):
        @pl.when(c > 0)
        def _():
            for at in range(2):

                def act(j, low, size, at=at):
                    held = windows[at].at[n, halo_rows(low, size)]
                    wait_on(held, halo_got.at[n, at, j])
                    pass_halo_copy(n, at, j, low, size).start()

                for_pieces(True, act)

    def turn(n, first, last):
        for i in range(first, last):
            turned[i] = keys_in[n, i * BLK : (i + 1) * BLK, :].T
            v_work[i] = values_in[n, i * BLK : (i + 1) * BLK, :]

    def turn_rows(n):
        for at in range(2):
            for other in range(pairs):
                j = 2 * other + 1 - side
                wait_on(windows[at].at[n, rows_of(j)], kv_got.at[n, at, j])
        turn(n, MAXDOC - 1, MAXDOC - 1 + blocks)

    def turn_halo(n):
        @pl.when(c > 0)
        def _():
            for at in range(2):

                def act(j, low, size, at=at):
                    held = windows[at].at[n, halo_rows(low, size)]
                    wait_on(held, halo_got.at[n, at, j])

                for_pieces(False, act)
            turn(n, 0, MAXDOC - 1)

        @pl.when(c == 0)
        def _():
            for ref in (turned, v_work):
                ref[0 : MAXDOC - 1] = jnp.zeros((MAXDOC - 1,) + ref.shape[1:], ref.dtype)

    causal = lax.broadcasted_iota(jnp.int32, (BLK, BLK), 1) <= lax.broadcasted_iota(
        jnp.int32, (BLK, BLK), 0
    )

    def side_columns(k):
        return pl.ds(aligned(lax.rem(k, 2) * HD), HD)

    def attend(k, slot):
        block = slot_block[slot]
        count = slot_count[slot]
        queries = q_work[block]
        keys = jnp.concatenate([turned[block + i] for i in range(MAXDOC)], axis=1)
        values = jnp.concatenate([v_work[block + i] for i in range(MAXDOC)], axis=0)
        scores = jnp.dot(queries, keys, preferred_element_type=jnp.float32)
        parts = [scores[:, i * BLK : (i + 1) * BLK] for i in range(MAXDOC)]
        for i in range(MAXDOC - 1):
            inside = jnp.full((BLK, BLK), count - (MAXDOC - 1 - i), jnp.int32) > 0
            parts[i] = jnp.where(inside, parts[i], -jnp.inf)
        parts[-1] = jnp.where(causal, parts[-1], -jnp.inf)
        top = jnp.max(functools.reduce(jnp.maximum, parts), axis=1, keepdims=True)
        parts = [jnp.exp2((x - top) * factor) for x in parts]
        total = jnp.sum(functools.reduce(jnp.add, parts), axis=1, keepdims=True)
        weights = jnp.concatenate([x.astype(jnp.bfloat16) for x in parts], axis=1)
        mixed = jnp.dot(weights, values, preferred_element_type=jnp.float32) / total
        out[lax.div(k, 2), slot, :, side_columns(k)] = mixed.astype(out.dtype)

    def owner(k):
        return 2 * pair + lax.div(lax.div(k, half), kv_heads)

    def column(k):
        n, i = lax.div(k, half), lax.rem(k, half)
        return lax.rem(n, kv_heads) * 2 * half + side * half + i

    def columns(col):
        return pl.ds(aligned(col * HD), HD)

    def target_of(s):
        away = nc // 2 + (1 - 2 * lax.rem(s, 2)) * lax.div(s + 1, 2)
        return lax.rem(c + away, nc)

    def send_out(k, s):
        t = target_of(s)
        col = column(k)
        slots_of = pl.ds(t * cap, cap)

        def send(src, where):
            pltpu.make_async_remote_copy(
                src_ref=src,
                dst_ref=got_ref.at[pl.ds(c * cap, cap), :, where],
                send_sem=out_sent.at[k],
                recv_sem=out_got.at[col],
                device_id=(t, owner(k)),
                device_id_type=MESH,
            ).start()

        @pl.when(k < half)
        def _():
            send(out.at[lax.div(k, 2), slots_of, :, side_columns(k)], columns(col))

        @pl.when((k >= half) & (lax.rem(k, 2) == 1))
        def _():
            send(out.at[lax.div(k, 2), slots_of], both_columns(col))

    def both_columns(col):
        return pl.ds(aligned((col - 1) * HD), 2 * HD)

    own_slots = pl.ds(c * cap, cap)

    def send_own(k):
        col = column(k)
        src = out.at[lax.div(k, 2), own_slots, :, side_columns(k)]
        dst = got_ref.at[own_slots, :, columns(col)]

        @pl.when(owner(k) == h)
        def _():
            pltpu.make_async_copy(src, dst, own_got.at[col]).start()

        @pl.when(owner(k) != h)
        def _():
            pltpu.make_async_remote_copy(
                src_ref=src,
                dst_ref=dst,
                send_sem=own_sent.at[k],
                recv_sem=own_got.at[col],
                device_id=(c, partner),
                device_id_type=MESH,
            ).start()

    def head_step(k):
        for j in range(nh):
            wait_on(q_in.at[k, pl.ds(j * part, part)], q_got.at[k, j])
        q_work[...] = q_in[k].reshape(q_work.shape)

        def target(s, carry):
            t = target_of(s)
            for r in range(cap):
                attend(k, t * cap + r)
                if r == 0:

                    @pl.when(s > 0)
                    def _():
                        send_out(k, s - 1)

            return carry

        lax.fori_loop(0, nc, target, 0)
        send_own(k)

    collect(0)
    turn_rows(0)
    pass_halo(0)
    turn_halo(0)

    def one(k, carry):
        n, i = lax.div(k, half), lax.rem(k, half)

        @pl.when((i == 0) & (n > 0))
        def _():
            turn_rows(n)
            turn_halo(n)

        head_step(k)
        def after(head, act):
            pl.when(k == head)(act)

        for later in range(2, shared):
            after(later - 2, functools.partial(lead, later, jnp.logical_not(odd)))
        for later in range(DIRECT, shared):
            after(later - DIRECT, functools.partial(relay, later))
            after(later, functools.partial(spread, later))

        @pl.when(k + AHEAD < heads)
        def _():
            send_q(k + AHEAD)

        for later in range(1, min(DIRECT, shared)):
            after(2 * later - 1, functools.partial(detour_on, later))
        for later in range(1, shared):
            after(2 * later - 2, functools.partial(collect, later))
            last = later * half - 1
            after(last - 1 if later == 1 else last, functools.partial(pass_halo, later))
        return carry

    lax.fori_loop(0, heads, one, 0)

    def settle_kv(n):
        for at in range(2):
            for d in range(pairs):
                wait_on(windows[at].at[n, rows_of(h)], kv_sent.at[n, at, d])
                if d:
                    pass_kv_copy(n, at, d).wait_send()

            @pl.when(c > 0)
            def _(at=at):
                for_pieces(True, lambda *p: pass_halo_copy(n, at, *p).wait_send())

            def sent(j, low, size, at=at):
                wait_on(windows[at].at[n, halo_rows(low, size)], halo_sent.at[n, at, j])

            @pl.when(has_next)
            def _(sent=sent):
                if n >= DIRECT:
                    for_own_pieces(sent)
                else:
                    for_pieces(True, sent)

        if 0 < n < DIRECT:

            @pl.when(relays)
            def _():
                def sent_on(j, low, size):
                    @pl.when(h != j)
                    def _():
                        wait_on(
                            via.at[1, n - 1, halo_rows(low, size)], via_sent.at[1, n - 1, j]
                        )

                for_pieces(True, sent_on)

        if n >= DIRECT:

            def for_places(act):
                for_own_pieces(
                    lambda *p: for_other_pairs(lambda at, d: act(at, place_of(n, d), *p))
                )

            def settled(buffer, sems):
                def act(at, q, j, low, size):
                    wait_on(buffer.at[at, q, halo_rows(low, size)], sems.at[at, q, j])

                return act

            for cond, buffer, sems in (
                (has_next, stage, away_sent),
                (relays, via, via_sent),
                (c > 0, stage, stage_sent),
            ):

                @pl.when(cond)
                def _(buffer=buffer, sems=sems):
                    for_places(settled(buffer, sems))

    for n in range(shared):
        settle_kv(n)

    mine_copy.wait()

    def drain(k, carry):
        for d in range(1, nh):
            wait_on(q_in.at[k, my_rows], q_sent.at[k, d])

        @pl.when(owner(k) != h)
        def _():
            wait_on(out.at[lax.div(k, 2), own_slots, :, side_columns(k)], own_sent.at[k])

        wait_on(got_ref.at[own_slots, :, columns(k)], own_got.at[k])
        others = pl.ds(0, (nc - 1) * cap)
        paired = lax.rem(k, 2) == 1

        @pl.when(k < half)
        def _():
            wait_on(out.at[lax.div(k, 2), others, :, side_columns(k)], out_sent.at[k])

        @pl.when((k >= half) & paired)
        def _():
            wait_on(out.at[lax.div(k, 2), others], out_sent.at[k])

        first_group = side * kv_heads + lax.div(k, 2 * half) == 0

        @pl.when(first_group)
        def _():
            wait_on(got_ref.at[others, :, columns(k)], out_got.at[k])

        @pl.when(jnp.logical_not(first_group) & paired)
        def _():
            wait_on(got_ref.at[others, :, both_columns(k)], out_got.at[k])

        return carry

    lax.fori_loop(0, heads, drain, 0)


def fused(doc_ids, plan, query, key, value):
    nc, nh = lax.axis_size("ctx"), lax.axis_size("head")
    part = query.shape[0]
    rows = nh * part
    blocks = rows // BLK
    heads = query.shape[1] // nh // HD
    kv_heads = key.shape[1] // nh // HD
    shared = 2 * kv_heads
    places = max(DIRECT - 1, (nh // 2 - 1) * (shared - DIRECT))
    cap = -(-blocks // nc)
    slots = nc * cap
    window = HALO + rows
    dma = pltpu.SemaphoreType.DMA
    buffers = [
        (shared, window, HD),
        (shared, window, HD),
        (2, places, HALO, HD),
        (2, places, HALO, HD),
        (heads, rows, HD),
        (blocks, BLK, HD),
        (window // BLK, HD, BLK),
        (window // BLK, BLK, HD),
        (heads // 2, slots, BLK, 2 * HD),
    ]
    held = 2 * sum(math.prod(shape) for shape in buffers)
    return pl.pallas_call(
        functools.partial(fused_kernel, kv_heads, cap),
        out_shape=[
            jax.ShapeDtypeStruct((slots, BLK, heads * HD), query.dtype),
            jax.ShapeDtypeStruct((blocks,), jnp.int32),
        ],
        in_specs=[pl.BlockSpec(memory_space=pltpu.HBM)] * 5,
        out_specs=[pl.BlockSpec(memory_space=pl.ANY)] * 2,
        scratch_shapes=[
            pltpu.SMEM(n, jnp.int32)
            for n in (doc_ids.shape, plan.shape, (blocks,), (slots,), (slots,))
        ]
        + [pltpu.VMEM(shape, query.dtype) for shape in buffers]
        + [dma((heads, nh))] * 2
        + [dma((shared, 2, nh))] * 6
        + [dma((2, places, nh))] * 5
        + [dma((heads,))] * 4
        + [dma((3,))]
        + [pltpu.SemaphoreType.REGULAR((nc.bit_length(), 2))],
        compiler_params=pltpu.CompilerParams(
            collective_id=0, has_side_effects=True, vmem_limit_bytes=held + (6 << 20)
        ),
        name="fused",
    )(doc_ids, plan, query, key, value)


def place_kernel(mine_ref, got_ref, o_ref, sems):
    copies = []
    for i in range(o_ref.shape[0] // BLK):
        copy = pltpu.make_async_copy(
            got_ref.at[mine_ref[i]], o_ref.at[pl.ds(i * BLK, BLK)], sems.at[i]
        )
        copy.start(priority=i % 2)
        copies.append(copy)
    for copy in copies:
        copy.wait()


def place(mine, got):
    blocks = mine.shape[0]
    width = got.shape[2]
    return pl.pallas_call(
        place_kernel,
        out_shape=jax.ShapeDtypeStruct((blocks * BLK, width), got.dtype),
        in_specs=[
            pl.BlockSpec(memory_space=pltpu.SMEM),
            pl.BlockSpec(memory_space=pl.ANY),
        ],
        out_specs=pl.BlockSpec(memory_space=pl.ANY),
        scratch_shapes=[pltpu.SemaphoreType.DMA((blocks,))],
        compiler_params=pltpu.CompilerParams(vmem_limit_bytes=1 << 20),
        name="place",
    )(mine, got)


def shards(query, key, value, doc_ids, plan):
    operands = [
        pltpu.with_memory_space_constraint(x, pltpu.HBM)
        for x in (doc_ids, plan, query, key, value)
    ]
    got, mine = fused(*operands)
    return place(mine, got)


def solution(mesh):
    return jax.shard_map(
        shards,
        mesh=mesh,
        in_specs=(
            P(("ctx", "head"), None),
            P(("ctx", "head"), None),
            P(("ctx", "head"), None),
            P(),
            P(),
        ),
        out_specs=P("ctx", "head"),
        check_vma=False,
    )
```
